512 devices in a mesh: hx: 32 (over x, z_lo), hy: 4 (over y), vz: 4 (over z_hi, core).
Axes of the slice: x: 4, y: 4, z: 16 (z_hi: 2, z_lo: 8; z = z_hi * 8 + z_lo), core: 2. Of those that a mesh axis runs over, the one named last changes fastest.
Arguments:
- prognostic: float32 [5, 80, 4, 4, 4, 4096], P(None, 'vz', None, None, 'hy', 'hx'), may hold values from -6 to 6
- metric: float32 [4, 4, 4, 4096], P(None, None, 'hy', 'hx'), may hold values from 0.5 to 2
- first_flux: float32 [5, 5], replicated, may hold values from -2.5 to 2.5
- second_flux: float32 [5, 5], replicated, may hold values from -2.5 to 2.5
- neighbour_face: int32 [4, 4, 4096], P(None, 'hy', 'hx'), may hold values from 0 to 3
- orientation: int32 [4, 4, 4096], P(None, 'hy', 'hx'), may hold values from 0 to 1
- coupling: float32 [4, 80, 4, 4, 4, 4096], P(None, None, 'vz', None, 'hy', 'hx'), may hold values from 0.1 to 1
- damping: float32 [4, 4, 4, 4096], P('vz', None, 'hy', 'hx'), may hold values from 0.005 to 0.05
Outputs:
- updated: float32 [5, 80, 4, 4, 4, 4096], P(None, 'vz', None, None, 'hy', 'hx')
The draws below stay inside these ranges and needn't reach their ends.
All inputs are finite; a program needn't handle non-finite values.
Results may differ from the reference program's by a relative error of at most 0.0003.
Values sent between devices are 32-bit elements; how exact they have to be, the bound alone decides.
A program may use at most 64 MiB of HBM per device.

```python
import math
import jax
import jax.numpy as jnp
import numpy as np
from jax import lax

FIELDS = 5
NODES = 4
FACES = 4
L = 80
NEX = 4
NEY = 4096


def place_ends(entries, rng, smallest, top_value):
    dims = entries.shape
    index_at = [jax.random.randint(jax.random.fold_in(rng, axis), (), 0, dims[axis]) for axis in range(len(dims))]
    entries = entries.at[tuple(index_at)].set(smallest)
    longest = dims.index(max(dims))
    index_at[longest] = (index_at[longest] + 1) % dims[longest]
    return entries.at[tuple(index_at)].set(top_value)


def levels(stream_key, extent, shards, least, largest):
    def one(position, blocks):
        draws = jax.random.uniform(jax.random.fold_in(jax.random.fold_in(stream_key, 6), position), (blocks,), jnp.float32, least / len(shards), largest / len(shards))
        return jnp.repeat(jnp.exp(draws), extent[position] // blocks).reshape((-1,) + (1,) * (len(extent) - position - 1))

    level = one(*shards[0])
    for cut in shards[1:]:
        level = level * one(*cut)
    return level


def noise(own_key, shape, spread, limit, cuts=(), kind=jnp.bfloat16):
    loudness = levels(own_key, shape, cuts, -0.22, 0.18) if cuts else 1.0
    entries = jax.random.normal(own_key, shape, jnp.float32) * spread * loudness
    return jnp.minimum(jnp.maximum(entries, -limit), limit).astype(kind)


def setup_inputs(seed: int = 0) -> dict:
    keys = jax.random.split(jax.random.key(seed), 9)
    return {
        "prognostic": noise(keys[0], (FIELDS, L, NODES, NODES, NEX, NEY), 1.0, 6.0, ((1, 4), (4, 4), (5, 32)), jnp.float32),
        "metric": jnp.clip(jnp.exp(math.log(2.0) - 1.3862944 * jax.random.uniform(keys[1], (NODES, NODES, NEX, NEY), jnp.float32) ** levels(keys[1], (NODES, NODES, NEX, NEY), ((2, 4), (3, 32)), -0.2, 0.2)), 0.5, 2.0),
        "first_flux": noise(keys[2], (FIELDS, FIELDS), FIELDS ** -0.5, 2.5, (), jnp.float32),
        "second_flux": noise(keys[3], (FIELDS, FIELDS), FIELDS ** -0.5, 2.5, (), jnp.float32),
        "neighbour_face": place_ends(jax.random.randint(keys[4], (FACES, NEX, NEY), 0, FACES), jax.random.fold_in(keys[4], 1), 0, FACES - 1).astype(jnp.int32),
        "orientation": place_ends(jax.random.randint(keys[5], (FACES, NEX, NEY), 0, 2), jax.random.fold_in(keys[5], 1), 0, 1).astype(jnp.int32),
        "coupling": jnp.clip(0.1 + 0.9 * jax.random.uniform(keys[6], (4, L, NODES, NODES, NEX, NEY), jnp.float32) ** levels(keys[6], (4, L, NODES, NODES, NEX, NEY), ((2, 4), (4, 4), (5, 32)), -0.2, 0.2), 0.1, 1.0),
        "damping": jnp.clip(jnp.exp(math.log(0.05) - 2.3025851 * jax.random.uniform(keys[7], (NODES, NODES, NEX, NEY), jnp.float32) ** levels(keys[7], (NODES, NODES, NEX, NEY), ((0, 4), (2, 4), (3, 32)), -0.2, 0.2)), 0.005, 0.05),
    }


step_size = 0.05
rusanov_speed = 1.0
lift_weight = 6.0
gravity_couple = 0.5
density_couple = 0.3
theta_couple = 0.4

def derivative_table():
    points = np.array([-1.0, -1.0 / np.sqrt(5.0), 1.0 / np.sqrt(5.0), 1.0])
    number = points.shape[0]
    barycentric = np.ones(number)
    for source in range(number):
        for another in range(number):
            if another != source:
                barycentric[source] = barycentric[source] / (points[source] - points[another])
    matrix = np.zeros((number, number))
    for target in range(number):
        for source in range(number):
            if target != source:
                matrix[target, source] = barycentric[source] / barycentric[target] / (points[target] - points[source])
        matrix[target, target] = -np.sum(matrix[target])
    return jnp.asarray(matrix, dtype=jnp.float32)

def face_traces(fields):
    west_face = fields[:, :, :, 0]
    east_face = fields[:, :, :, -1]
    south_face = fields[:, :, 0, :]
    north_face = fields[:, :, -1, :]
    return jnp.stack([west_face, east_face, south_face, north_face], axis=2)

def pick_face(candidates, table_row, flip_row):
    chosen = jnp.zeros(candidates.shape[:2] + candidates.shape[3:], candidates.dtype)
    for option in range(candidates.shape[2]):
        chosen = chosen + jnp.where(table_row == option, candidates[:, :, option], 0.0)
    reverse = chosen[:, :, ::-1]
    return jnp.where(flip_row == 1, reverse, chosen)

def section_values(fields, outer_traces, metric, first_flux, second_flux):
    derivative = derivative_table()
    highest = lax.Precision.HIGHEST
    flux_first = jnp.einsum('fg,gljiab->fljiab', first_flux, fields, precision=highest)
    flux_second = jnp.einsum('fg,gljiab->fljiab', second_flux, fields, precision=highest)
    divergence = jnp.einsum('ci,fljiab->fljcab', derivative, flux_first, precision=highest)
    divergence = divergence + jnp.einsum('cj,fljiab->flciab', derivative, flux_second, precision=highest)
    own_traces = face_traces(fields)
    own_first = face_traces(flux_first)
    own_second = face_traces(flux_second)
    own_normal = jnp.stack([-own_first[:, :, 0], own_first[:, :, 1], -own_second[:, :, 2], own_second[:, :, 3]], axis=2)
    outer_first = jnp.einsum('fg,glhkab->flhkab', first_flux, outer_traces[:, :, 0:2], precision=highest)
    outer_second = jnp.einsum('fg,glhkab->flhkab', second_flux, outer_traces[:, :, 2:4], precision=highest)
    outer_normal = jnp.concatenate([-outer_first[:, :, 0:1], outer_first[:, :, 1:2], -outer_second[:, :, 0:1], outer_second[:, :, 1:2]], axis=2)
    correction = 0.5 * (own_normal - outer_normal) + 0.5 * rusanov_speed * (outer_traces - own_traces)
    blank_face = jnp.zeros_like(correction[:, :, 0])
    middle_blanks = [blank_face] * (fields.shape[3] - 2)
    across_first = jnp.stack([correction[:, :, 0]] + middle_blanks + [correction[:, :, 1]], axis=3)
    across_second = jnp.stack([correction[:, :, 2]] + middle_blanks + [correction[:, :, 3]], axis=2)
    tendency = metric * (lift_weight * (across_first + across_second) - divergence)
    return fields + step_size * tendency

def level_difference(column_values):
    upper_part = jnp.concatenate([column_values[1:], jnp.zeros_like(column_values[:1])], axis=0)
    lower_part = jnp.concatenate([jnp.zeros_like(column_values[:1]), column_values[:-1]], axis=0)
    return upper_part - lower_part

def column_solve(entry_a, entry_b, centre, entry_d, entry_e, source):
    empty_row = jnp.zeros_like(source[0])

    def forward(carried, level_row):
        far_ratio, far_second, far_value, near_ratio, near_second, near_value = carried
        lower_two, lower_one, middle, upper_one, upper_two, given_value = level_row
        reduced = lower_one - lower_two * far_ratio
        pivot_entry = middle - lower_two * far_second - reduced * near_ratio
        upper_ratio = (upper_one - reduced * near_second) / pivot_entry
        second_ratio = upper_two / pivot_entry
        scaled_value = (given_value - lower_two * far_value - reduced * near_value) / pivot_entry
        return ((near_ratio, near_second, near_value, upper_ratio, second_ratio, scaled_value), (upper_ratio, second_ratio, scaled_value))
    initial = (empty_row, empty_row, empty_row, empty_row, empty_row, empty_row)
    unused, (ratios, seconds, scaled) = lax.scan(forward, initial, (entry_a, entry_b, centre, entry_d, entry_e, source))

    def backward(carried, level_row):
        next_one, next_two = carried
        upper_ratio, second_ratio, scaled_value = level_row
        solved = scaled_value - upper_ratio * next_one - second_ratio * next_two
        return ((solved, next_one), solved)
    unused, solution = lax.scan(backward, (empty_row, empty_row), (ratios, seconds, scaled), reverse=True)
    return solution

def reference(prognostic, metric, first_flux, second_flux, neighbour_face, orientation, coupling, damping):

    def one_level(level_fields):
        fields = level_fields[:, None]
        own_traces = face_traces(fields)
        candidates = [jnp.roll(own_traces, 1, axis=4), jnp.roll(own_traces, -1, axis=4), jnp.roll(own_traces, 1, axis=5), jnp.roll(own_traces, -1, axis=5)]
        outer_traces = jnp.stack([pick_face(candidates[face_index], neighbour_face[face_index], orientation[face_index]) for face_index in range(4)], axis=2)
        return section_values(fields, outer_traces, metric, first_flux, second_flux)[:, 0]
    section_state = jnp.moveaxis(lax.map(one_level, jnp.moveaxis(prognostic, 1, 0)), 0, 1)
    source = section_state[3] - gravity_couple * level_difference(section_state[4])
    centre = coupling[0] + coupling[1] + coupling[2] + coupling[3] + damping[None]
    vertical_speed = column_solve(-coupling[0], -coupling[1], centre, -coupling[2], -coupling[3], source)
    speed_jump = level_difference(vertical_speed)
    return jnp.stack([section_state[0] - density_couple * speed_jump, section_state[1], section_state[2], vertical_speed, section_state[4] - theta_couple * speed_jump])
```

```python
import functools

import jax
import jax.numpy as jnp
import numpy as np
from jax import lax
from jax.experimental import pallas as pl
from jax.experimental.pallas import tpu as pltpu
from jax.sharding import PartitionSpec as P

step_size = 0.05
lift_weight = 6.0
gravity_couple = 0.5
density_couple = 0.3
theta_couple = 0.4

FIELDS = 5
ROWS = 8
LANES = 128


def derivative_matrix():
    points = np.array([-1.0, -1.0 / np.sqrt(5.0), 1.0 / np.sqrt(5.0), 1.0])
    number = points.shape[0]
    barycentric = np.ones(number)
    for source in range(number):
        for another in range(number):
            if another != source:
                barycentric[source] = barycentric[source] / (points[source] - points[another])
    matrix = np.zeros((number, number))
    for target in range(number):
        for source in range(number):
            if target != source:
                matrix[target, source] = (
                    barycentric[source] / barycentric[target] / (points[target] - points[source])
                )
        matrix[target, target] = -np.sum(matrix[target])
    return matrix


def weight_table():
    d = derivative_matrix()
    half = 0.5 * lift_weight
    along = np.zeros((7, ROWS))
    for row in range(ROWS):
        i = row % 4
        for offset in range(-3, 4):
            if 0 <= i + offset < 4:
                along[offset + 3, row] = -d[i, i + offset]
    cx = np.array([{0: -half, 3: half}.get(r % 4, 0.0) for r in range(ROWS)])
    along[3] += cx
    across = np.zeros((2, 2, 2, ROWS))
    for tile in range(2):
        for other in range(2):
            for row in range(ROWS):
                jl = row // 4
                j = 2 * tile + jl
                across[tile, other, 0, row] = -d[j, 2 * other + jl]
                across[tile, other, 1, row] = -d[j, 2 * other + 1 - jl]
    cy = np.zeros((2, ROWS))
    cy[0, :4] = -half
    cy[1, 4:] = half
    for tile in range(2):
        across[tile, tile, 0] += cy[tile]
    own = np.zeros((2, ROWS))
    for tile in range(2):
        own[tile] = -np.abs(cx) - np.abs(cy[tile])
    rows = np.concatenate(
        [along, across.reshape(8, ROWS), cx[None], np.abs(cx)[None], cy, np.abs(cy), own]
    )
    return np.ascontiguousarray(
        np.broadcast_to(rows[:, :, None], rows.shape + (LANES,)).astype(np.float32)
    )


def rows_of(shape=(ROWS, LANES)):
    return lax.broadcasted_iota(jnp.int32, shape, 0)


def lanes_of(shape=(ROWS, LANES)):
    return lax.broadcasted_iota(jnp.int32, shape, 1)


def spread(row):
    return jnp.broadcast_to(row, (ROWS, LANES))


def node_rows(face, flip):
    k = rows_of() % 4
    k = jnp.where(flip == 1, 3 - k, k)
    return jnp.where(
        face == 0, 4 * k, jnp.where(face == 1, 4 * k + 3, jnp.where(face == 2, k, 12 + k))
    )


def take_rows(tile, index):
    return jnp.take_along_axis(tile, index, axis=0, mode="promise_in_bounds")


def take_nodes(low, high, node):
    index = jnp.where(node >= ROWS, node - ROWS, node)
    return jnp.where(node >= ROWS, take_rows(high, index), take_rows(low, index))


def halves(low, high):
    return jnp.where(rows_of() < 4, low, high)


def pack_faces(state, tables, north_message, south_message):
    levels = state.shape[1]
    node = halves(
        node_rows(spread(tables[0:1]), spread(tables[1:2])),
        node_rows(spread(tables[2:3]), spread(tables[3:4])),
    )

    def at(count, carry):
        for field in range(FIELDS):
            chosen = take_nodes(
                state[field, count, 0:ROWS], state[field, count, ROWS : 2 * ROWS], node
            )
            north_message[field, count] = chosen[0:4]
            south_message[field, count] = chosen[4:8]
        return carry

    lax.fori_loop(0, levels, at, 0, unroll=2)


def pack_edges(state, edges):
    levels = state.shape[1]
    lane = lanes_of()
    zero = state[0, 0, 0:ROWS] - state[0, 0, 0:ROWS]

    def at(count, held):
        held = list(held)
        for field in range(FIELDS):
            number = field * levels + count
            at_first = lane == number
            at_last = lane == lax.rem(number + LANES - 1, LANES)
            for tile in range(2):
                moved = pltpu.roll(
                    state[field, count, tile * ROWS : (tile + 1) * ROWS], number, 1
                )
                held[tile] = jnp.where(at_first, moved, held[tile])
                held[2 + tile] = jnp.where(at_last, moved, held[2 + tile])
        return tuple(held)

    held = lax.fori_loop(0, levels, at, (zero,) * 4)
    for tile in range(2):
        edges[0, tile * ROWS : (tile + 1) * ROWS] = held[tile]
        edges[1, tile * ROWS : (tile + 1) * ROWS] = held[2 + tile]


def edge_values(before, after, faces, flips):
    def lane_value(table, row, lane):
        return jnp.broadcast_to(table[row : row + 1, lane : lane + 1], (ROWS, LANES))

    from_before = take_nodes(
        before[0:ROWS],
        before[ROWS : 2 * ROWS],
        node_rows(lane_value(faces, 2, 0), lane_value(flips, 2, 0)),
    )
    from_after = take_nodes(
        after[0:ROWS],
        after[ROWS : 2 * ROWS],
        node_rows(lane_value(faces, 3, LANES - 1), lane_value(flips, 3, LANES - 1)),
    )
    return halves(pltpu.roll(from_before, 1, 1), pltpu.roll(from_after, LANES - 1, 1))


def make_section(
    state, scale, first, second, faces, flips, west, east, before, after, weights, section
):
    levels = state.shape[1]
    row, lane = rows_of(), lanes_of()
    node = halves(
        node_rows(
            pltpu.roll(spread(faces[2:3]), LANES - 1, 1),
            pltpu.roll(spread(flips[2:3]), LANES - 1, 1),
        ),
        node_rows(pltpu.roll(spread(faces[3:4]), 1, 1), pltpu.roll(spread(flips[3:4]), 1, 1)),
    )
    edge = edge_values(before, after, faces, flips)
    at_edge = ((row < 4) & (lane == 0)) | ((row >= 4) & (lane == LANES - 1))
    left = row % 4 < 2
    place = [jnp.where(left, 2 * tile + row // 4, 4 + 2 * tile + row // 4) for tile in range(2)]

    def at(count, carry):
        q1 = [[None] * 2 for _ in range(FIELDS)]
        q2 = [[None] * 2 for _ in range(FIELDS)]
        rest = [[None] * 2 for _ in range(FIELDS)]
        own = [[None] * 2 for _ in range(FIELDS)]
        for field in range(FIELDS):
            number = field * levels + count
            tiles = [state[field, count, t * ROWS : (t + 1) * ROWS] for t in range(2)]
            swapped = [pltpu.roll(tile, 4, 0) for tile in tiles]
            chosen = take_nodes(tiles[0], tiles[1], node)
            across = halves(pltpu.roll(chosen, 1, 1), pltpu.roll(chosen, LANES - 1, 1))
            shift = lax.rem(2 * LANES - number, LANES)
            across = jnp.where(at_edge, pltpu.roll(edge, shift, 1), across)
            sides = jnp.concatenate([west[field, count], east[field, count]], axis=0)
            for t in range(2):
                along = take_rows(sides, place[t])
                total = weights[3] * tiles[t] - weights[15] * along
                for offset in (-3, -2, -1, 1, 2, 3):
                    total += weights[offset + 3] * pltpu.roll(tiles[t], (-offset) % ROWS, 0)
                q1[field][t] = total
                total = -weights[17 + t] * across
                for other in range(2):
                    total += weights[7 + 4 * t + 2 * other] * tiles[other]
                    total += weights[8 + 4 * t + 2 * other] * swapped[other]
                q2[field][t] = total
                rest[field][t] = (
                    weights[21 + t] * tiles[t] + weights[16] * along + weights[19 + t] * across
                )
                own[field][t] = tiles[t]
        for field in range(FIELDS):
            for t in range(2):
                total = rest[field][t]
                for other in range(FIELDS):
                    total += first[field, other] * q1[other][t]
                    total += second[field, other] * q2[other][t]
                section[field, count, t * ROWS : (t + 1) * ROWS] = (
                    own[field][t] + step_size * scale[t * ROWS : (t + 1) * ROWS] * total
                )
        return carry

    lax.fori_loop(0, levels, at, 0)


def column_message(section, message):
    levels = section.shape[1]
    for t in range(2):
        span = slice(t * ROWS, (t + 1) * ROWS)
        warm = [section[4, count, span] for count in range(levels)]
        entries = []
        for count in range(levels):
            total = section[3, count, span]
            if count + 1 < levels:
                total = total - gravity_couple * warm[count + 1]
            if count > 0:
                total = total + gravity_couple * warm[count - 1]
            entries.append(total)
        entries += [warm[0], warm[levels - 1]]
        for count, entry in enumerate(entries):
            message[2 * t, count] = entry[0:4]
            message[2 * t + 1, count] = entry[4:8]


def pair(low, high):
    return jnp.concatenate([low, high], axis=0)


def factor(coupling, damping, factors):
    levels = coupling.shape[1]
    half = levels // 2
    damp = pair(damping[...], damping[...])
    zero = damp - damp

    def at(t, carry):
        far_ratio, far_second, near_ratio, near_second = carry
        up = levels - 1 - t
        entry_a = pair(coupling[0, t], coupling[3, up])
        entry_b = pair(coupling[1, t], coupling[2, up])
        entry_d = pair(coupling[2, t], coupling[1, up])
        entry_e = pair(coupling[3, t], coupling[0, up])
        centre = entry_a + entry_b + entry_d + entry_e + damp
        reduced = entry_a * far_ratio - entry_b
        pivot = centre + entry_a * far_second - reduced * near_ratio
        inverse = 1.0 / pivot
        ratio = -(entry_d + reduced * near_second) * inverse
        second = -entry_e * inverse
        factors[0, t] = inverse
        factors[1, t] = entry_a * inverse
        factors[2, t] = reduced * inverse
        factors[3, t] = ratio
        factors[4, t] = second
        return near_ratio, near_second, ratio, second

    lax.fori_loop(0, half, at, (zero,) * 4)


def solve(factors, columns, message):
    parts, count = columns.shape[0], columns.shape[1] - 2
    levels = parts * count
    half = levels // 2

    def source(level):
        d, place = level // count, level % count
        entry = columns[d, place]
        if place == 0 and d > 0:
            entry = entry + gravity_couple * columns[d - 1, count + 1]
        if place == count - 1 and d < parts - 1:
            entry = entry - gravity_couple * columns[d + 1, count]
        return entry

    far = near = jnp.zeros((ROWS, LANES), jnp.float32)
    scaled = []
    for t in range(half):
        entry = pair(source(t), source(levels - 1 - t)) * factors[0, t]
        far, near = near, (entry + factors[1, t] * far) - factors[2, t] * near
        scaled.append(near)
    top, under = half - 1, half - 2
    value_1, value_2 = scaled[top], scaled[under]
    ratio_1, ratio_2 = factors[3, top], factors[3, under]
    second_1, second_2 = factors[4, top], factors[4, under]
    other_value = pltpu.roll(value_2, 4, 0)
    other_ratio = pltpu.roll(ratio_2, 4, 0)
    other_second = pltpu.roll(second_2, 4, 0)
    here = 1.0 - second_1 * other_second
    there = ratio_1 - second_1 * other_ratio
    right = value_1 - second_1 * other_value
    here_2 = pltpu.roll(here, 4, 0)
    there_2 = pltpu.roll(there, 4, 0)
    right_2 = pltpu.roll(right, 4, 0)
    mine = (right * here_2 - there * right_2) / (here * here_2 - there * there_2)
    next_one, next_two = mine, pltpu.roll(mine, 4, 0)
    blank = jnp.zeros((4, LANES), jnp.float32)

    def put(level, entry):
        for d in range(parts):
            place = level - d * count + 1
            if 0 <= place < count + 2:
                message[d, place] = entry

    put(-1, blank)
    put(levels, blank)
    put(top, mine[0:4])
    put(levels - 1 - top, mine[4:8])
    for t in range(half - 2, -1, -1):
        found = (scaled[t] - factors[4, t] * next_two) - factors[3, t] * next_one
        put(t, found[0:4])
        put(levels - 1 - t, found[4:8])
        next_one, next_two = found, next_one


def finish(section, returned, updated):
    levels = section.shape[1]

    def at(count, carry):
        for t in range(2):
            span = slice(t * ROWS, (t + 1) * ROWS)

            def level(place):
                return pair(returned[2 * t, place], returned[2 * t + 1, place])

            jump = level(count + 2) - level(count)
            updated[0, count, span] = section[0, count, span] - density_couple * jump
            updated[1, count, span] = section[1, count, span]
            updated[2, count, span] = section[2, count, span]
            updated[3, count, span] = level(count + 1)
            updated[4, count, span] = section[4, count, span] - theta_couple * jump
        return carry

    lax.fori_loop(0, levels, at, 0, unroll=2)


VM = pl.BlockSpec(memory_space=pltpu.VMEM)
SM = pl.BlockSpec(memory_space=pltpu.SMEM)


def f32(*shape):
    return jax.ShapeDtypeStruct(shape, jnp.float32)


def pack_kernel(state, tables, north_message, south_message, edges):
    pack_faces(state, tables[...], north_message, south_message)
    pack_edges(state, edges)


def section_kernel(
    first, second, state, scale, faces, flips, west, east, before, after, weights, section, message
):
    make_section(
        state,
        scale,
        first,
        second,
        faces[...],
        flips[...],
        west,
        east,
        before[...],
        after[...],
        weights,
        section,
    )
    column_message(section, message)


def per_device(
    prognostic, metric, first_flux, second_flux, neighbour_face, orientation, coupling, damping
):
    levels = prognostic.shape[1]
    parts = lax.axis_size("vz")
    state = prognostic.reshape(FIELDS, levels, 16, LANES)
    scale = metric.reshape(16, LANES)
    faces = neighbour_face.reshape(4, LANES)
    flips = orientation.reshape(4, LANES)
    couples = coupling.reshape(4, levels * parts, 4, LANES)
    damp = damping.reshape(4, LANES)

    def shifted(x, axis, by):
        size = lax.axis_size(axis)
        return lax.ppermute(x, axis, [(i, (i + by) % size) for i in range(size)])

    west_table = shifted(jnp.stack([faces[0], flips[0]]), "hy", -1)
    east_table = shifted(jnp.stack([faces[1], flips[1]]), "hy", 1)
    tables = jnp.concatenate([west_table, east_table])
    factors = pl.pallas_call(
        factor,
        out_shape=f32(5, levels * parts // 2, ROWS, LANES),
        in_specs=[VM, VM],
        out_specs=VM,
        name="factor",
        cost_estimate=pl.CostEstimate(flops=4000000, bytes_accessed=1500000, transcendentals=0),
    )(couples, damp)
    north_message, south_message, edges = pl.pallas_call(
        pack_kernel,
        out_shape=(f32(FIELDS, levels, 4, LANES), f32(FIELDS, levels, 4, LANES), f32(2, 16, LANES)),
        in_specs=[VM, VM],
        out_specs=(VM, VM, VM),
        name="pack",
    )(state, tables)
    after = shifted(edges[0], "hx", -1)
    before = shifted(edges[1], "hx", 1)
    west = shifted(north_message, "hy", 1)
    east = shifted(south_message, "hy", -1)
    section, message = pl.pallas_call(
        section_kernel,
        out_shape=(f32(FIELDS, levels, 16, LANES), f32(parts, levels + 2, 4, LANES)),
        in_specs=[SM, SM] + [VM] * 9,
        out_specs=(VM, VM),
        name="section",
    )(
        first_flux,
        second_flux,
        state,
        scale,
        faces,
        flips,
        west,
        east,
        before,
        after,
        jnp.asarray(weight_table()),
    )
    columns = lax.all_to_all(message, "vz", split_axis=0, concat_axis=0, tiled=True)
    back = pl.pallas_call(
        solve,
        out_shape=f32(parts, levels + 2, 4, LANES),
        in_specs=[VM, VM],
        out_specs=VM,
        name="solve",
    )(factors, columns)
    returned = lax.all_to_all(back, "vz", split_axis=0, concat_axis=0, tiled=True)
    updated = pl.pallas_call(
        finish,
        out_shape=f32(FIELDS, levels, 16, LANES),
        in_specs=[VM, VM],
        out_specs=VM,
        name="finish",
    )(section, returned)
    return updated.reshape(prognostic.shape)


def solution(mesh):
    placed = (
        P(None, "vz", None, None, "hy", "hx"),
        P(None, None, "hy", "hx"),
        P(),
        P(),
        P(None, "hy", "hx"),
        P(None, "hy", "hx"),
        P(None, None, "vz", None, "hy", "hx"),
        P("vz", None, "hy", "hx"),
    )
    return jax.shard_map(
        per_device,
        mesh=mesh,
        in_specs=placed,
        out_specs=P(None, "vz", None, None, "hy", "hx"),
        check_vma=False,
    )
```

```python
import functools

import jax
import jax.numpy as jnp
import numpy as np
from jax import lax
from jax.experimental import pallas as pl
from jax.experimental.pallas import tpu as pltpu
from jax.sharding import PartitionSpec as P

step_size = 0.05
lift_weight = 6.0
gravity_couple = 0.5
density_couple = 0.3
theta_couple = 0.4

FIELDS = 5
ROWS = 8
LANES = 128


def derivative_matrix():
    points = np.array([-1.0, -1.0 / np.sqrt(5.0), 1.0 / np.sqrt(5.0), 1.0])
    number = points.shape[0]
    barycentric = np.ones(number)
    for source in range(number):
        for another in range(number):
            if another != source:
                barycentric[source] = barycentric[source] / (points[source] - points[another])
    matrix = np.zeros((number, number))
    for target in range(number):
        for source in range(number):
            if target != source:
                matrix[target, source] = (
                    barycentric[source] / barycentric[target] / (points[target] - points[source])
                )
        matrix[target, target] = -np.sum(matrix[target])
    return matrix


def weight_table():
    d = derivative_matrix()
    half = 0.5 * lift_weight
    along = np.zeros((7, ROWS))
    for row in range(ROWS):
        i = row % 4
        for offset in range(-3, 4):
            if 0 <= i + offset < 4:
                along[offset + 3, row] = -d[i, i + offset]
    cx = np.array([{0: -half, 3: half}.get(r % 4, 0.0) for r in range(ROWS)])
    along[3] += cx
    across = np.zeros((2, 2, 2, ROWS))
    for tile in range(2):
        for other in range(2):
            for row in range(ROWS):
                jl = row // 4
                j = 2 * tile + jl
                across[tile, other, 0, row] = -d[j, 2 * other + jl]
                across[tile, other, 1, row] = -d[j, 2 * other + 1 - jl]
    cy = np.zeros((2, ROWS))
    cy[0, :4] = -half
    cy[1, 4:] = half
    for tile in range(2):
        across[tile, tile, 0] += cy[tile]
    own = np.zeros((2, ROWS))
    for tile in range(2):
        own[tile] = -np.abs(cx) - np.abs(cy[tile])
    rows = np.concatenate(
        [along, across.reshape(8, ROWS), cx[None], np.abs(cx)[None], cy, np.abs(cy), own]
    )
    return np.ascontiguousarray(
        np.broadcast_to(rows[:, :, None], rows.shape + (LANES,)).astype(np.float32)
    )


def rows_of(shape=(ROWS, LANES)):
    return lax.broadcasted_iota(jnp.int32, shape, 0)


def lanes_of(shape=(ROWS, LANES)):
    return lax.broadcasted_iota(jnp.int32, shape, 1)


def spread(row):
    return jnp.broadcast_to(row, (ROWS, LANES))


def node_rows(face, flip):
    k = rows_of() % 4
    k = jnp.where(flip == 1, 3 - k, k)
    return jnp.where(
        face == 0, 4 * k, jnp.where(face == 1, 4 * k + 3, jnp.where(face == 2, k, 12 + k))
    )


def take_rows(tile, index):
    return jnp.take_along_axis(tile, index, axis=0, mode="promise_in_bounds")


def take_nodes(low, high, node):
    index = jnp.where(node >= ROWS, node - ROWS, node)
    return jnp.where(node >= ROWS, take_rows(high, index), take_rows(low, index))


def halves(low, high):
    return jnp.where(rows_of() < 4, low, high)


def pack_faces(state, tables, north_message, south_message):
    levels = state.shape[1]
    node = halves(
        node_rows(spread(tables[0:1]), spread(tables[1:2])),
        node_rows(spread(tables[2:3]), spread(tables[3:4])),
    )

    def at(count, carry):
        for field in range(FIELDS):
            chosen = take_nodes(
                state[field, count, 0:ROWS], state[field, count, ROWS : 2 * ROWS], node
            )
            north_message[field, count] = chosen[0:4]
            south_message[field, count] = chosen[4:8]
        return carry

    lax.fori_loop(0, levels, at, 0, unroll=2)


def pack_edges(state, edges):
    levels = state.shape[1]
    lane = lanes_of()
    zero = state[0, 0, 0:ROWS] - state[0, 0, 0:ROWS]

    def at(count, held):
        held = list(held)
        for field in range(FIELDS):
            number = field * levels + count
            at_first = lane == number
            at_last = lane == lax.rem(number + LANES - 1, LANES)
            for tile in range(2):
                moved = pltpu.roll(
                    state[field, count, tile * ROWS : (tile + 1) * ROWS], number, 1
                )
                held[tile] = jnp.where(at_first, moved, held[tile])
                held[2 + tile] = jnp.where(at_last, moved, held[2 + tile])
        return tuple(held)

    held = lax.fori_loop(0, levels, at, (zero,) * 4)
    for tile in range(2):
        edges[0, tile * ROWS : (tile + 1) * ROWS] = held[tile]
        edges[1, tile * ROWS : (tile + 1) * ROWS] = held[2 + tile]


def edge_values(before, after, faces, flips):
    def lane_value(table, row, lane):
        return jnp.broadcast_to(table[row : row + 1, lane : lane + 1], (ROWS, LANES))

    from_before = take_nodes(
        before[0:ROWS],
        before[ROWS : 2 * ROWS],
        node_rows(lane_value(faces, 2, 0), lane_value(flips, 2, 0)),
    )
    from_after = take_nodes(
        after[0:ROWS],
        after[ROWS : 2 * ROWS],
        node_rows(lane_value(faces, 3, LANES - 1), lane_value(flips, 3, LANES - 1)),
    )
    return halves(pltpu.roll(from_before, 1, 1), pltpu.roll(from_after, LANES - 1, 1))


def make_section(
    state, scale, first, second, faces, flips, west, east, before, after, weights, section
):
    levels = state.shape[1]
    row, lane = rows_of(), lanes_of()
    node = halves(
        node_rows(
            pltpu.roll(spread(faces[2:3]), LANES - 1, 1),
            pltpu.roll(spread(flips[2:3]), LANES - 1, 1),
        ),
        node_rows(pltpu.roll(spread(faces[3:4]), 1, 1), pltpu.roll(spread(flips[3:4]), 1, 1)),
    )
    edge = edge_values(before, after, faces, flips)
    at_edge = ((row < 4) & (lane == 0)) | ((row >= 4) & (lane == LANES - 1))
    left = row % 4 < 2
    place = [jnp.where(left, 2 * tile + row // 4, 4 + 2 * tile + row // 4) for tile in range(2)]

    def at(count, carry):
        q1 = [[None] * 2 for _ in range(FIELDS)]
        q2 = [[None] * 2 for _ in range(FIELDS)]
        rest = [[None] * 2 for _ in range(FIELDS)]
        own = [[None] * 2 for _ in range(FIELDS)]
        for field in range(FIELDS):
            number = field * levels + count
            tiles = [state[field, count, t * ROWS : (t + 1) * ROWS] for t in range(2)]
            swapped = [pltpu.roll(tile, 4, 0) for tile in tiles]
            chosen = take_nodes(tiles[0], tiles[1], node)
            across = halves(pltpu.roll(chosen, 1, 1), pltpu.roll(chosen, LANES - 1, 1))
            shift = lax.rem(2 * LANES - number, LANES)
            across = jnp.where(at_edge, pltpu.roll(edge, shift, 1), across)
            sides = jnp.concatenate([west[field, count], east[field, count]], axis=0)
            for t in range(2):
                along = take_rows(sides, place[t])
                total = weights[3] * tiles[t] - weights[15] * along
                for offset in (-3, -2, -1, 1, 2, 3):
                    total += weights[offset + 3] * pltpu.roll(tiles[t], (-offset) % ROWS, 0)
                q1[field][t] = total
                total = -weights[17 + t] * across
                for other in range(2):
                    total += weights[7 + 4 * t + 2 * other] * tiles[other]
                    total += weights[8 + 4 * t + 2 * other] * swapped[other]
                q2[field][t] = total
                rest[field][t] = (
                    weights[21 + t] * tiles[t] + weights[16] * along + weights[19 + t] * across
                )
                own[field][t] = tiles[t]
        for field in range(FIELDS):
            for t in range(2):
                total = rest[field][t]
                for other in range(FIELDS):
                    total += first[field, other] * q1[other][t]
                    total += second[field, other] * q2[other][t]
                section[field, count, t * ROWS : (t + 1) * ROWS] = (
                    own[field][t] + step_size * scale[t * ROWS : (t + 1) * ROWS] * total
                )
        return carry

    lax.fori_loop(0, levels, at, 0)


def column_message(section, message):
    levels = section.shape[1]
    for t in range(2):
        span = slice(t * ROWS, (t + 1) * ROWS)
        warm = [section[4, count, span] for count in range(levels)]
        entries = []
        for count in range(levels):
            total = section[3, count, span]
            if count + 1 < levels:
                total = total - gravity_couple * warm[count + 1]
            if count > 0:
                total = total + gravity_couple * warm[count - 1]
            entries.append(total)
        entries += [warm[0], warm[levels - 1]]
        for count, entry in enumerate(entries):
            message[2 * t, count] = entry[0:4]
            message[2 * t + 1, count] = entry[4:8]


def pair(low, high):
    return jnp.concatenate([low, high], axis=0)


def factor(coupling, damping, factors):
    levels = coupling.shape[1]
    half = levels // 2
    damp = pair(damping[...], damping[...])
    zero = damp - damp

    def at(t, carry):
        far_ratio, far_second, near_ratio, near_second = carry
        up = levels - 1 - t
        entry_a = pair(coupling[0, t], coupling[3, up])
        entry_b = pair(coupling[1, t], coupling[2, up])
        entry_d = pair(coupling[2, t], coupling[1, up])
        entry_e = pair(coupling[3, t], coupling[0, up])
        centre = entry_a + entry_b + entry_d + entry_e + damp
        reduced = entry_a * far_ratio - entry_b
        pivot = centre + entry_a * far_second - reduced * near_ratio
        inverse = 1.0 / pivot
        ratio = -(entry_d + reduced * near_second) * inverse
        second = -entry_e * inverse
        factors[0, t] = inverse
        factors[1, t] = entry_a * inverse
        factors[2, t] = reduced * inverse
        factors[3, t] = ratio
        factors[4, t] = second
        return near_ratio, near_second, ratio, second

    lax.fori_loop(0, half, at, (zero,) * 4)


def solve(factors, columns, message):
    parts, count = columns.shape[0], columns.shape[1] - 2
    levels = parts * count
    half = levels // 2

    def source(level):
        d, place = level // count, level % count
        entry = columns[d, place]
        if place == 0 and d > 0:
            entry = entry + gravity_couple * columns[d - 1, count + 1]
        if place == count - 1 and d < parts - 1:
            entry = entry - gravity_couple * columns[d + 1, count]
        return entry

    far = near = jnp.zeros((ROWS, LANES), jnp.float32)
    scaled = []
    for t in range(half):
        entry = pair(source(t), source(levels - 1 - t)) * factors[0, t]
        far, near = near, (entry + factors[1, t] * far) - factors[2, t] * near
        scaled.append(near)
    top, under = half - 1, half - 2
    value_1, value_2 = scaled[top], scaled[under]
    ratio_1, ratio_2 = factors[3, top], factors[3, under]
    second_1, second_2 = factors[4, top], factors[4, under]
    other_value = pltpu.roll(value_2, 4, 0)
    other_ratio = pltpu.roll(ratio_2, 4, 0)
    other_second = pltpu.roll(second_2, 4, 0)
    here = 1.0 - second_1 * other_second
    there = ratio_1 - second_1 * other_ratio
    right = value_1 - second_1 * other_value
    here_2 = pltpu.roll(here, 4, 0)
    there_2 = pltpu.roll(there, 4, 0)
    right_2 = pltpu.roll(right, 4, 0)
    mine = (right * here_2 - there * right_2) / (here * here_2 - there * there_2)
    next_one, next_two = mine, pltpu.roll(mine, 4, 0)
    blank = jnp.zeros((4, LANES), jnp.float32)

    def put(level, entry):
        for d in range(parts):
            place = level - d * count + 1
            if 0 <= place < count + 2:
                message[d, place] = entry

    put(-1, blank)
    put(levels, blank)
    put(top, mine[0:4])
    put(levels - 1 - top, mine[4:8])
    for t in range(half - 2, -1, -1):
        found = (scaled[t] - factors[4, t] * next_two) - factors[3, t] * next_one
        put(t, found[0:4])
        put(levels - 1 - t, found[4:8])
        next_one, next_two = found, next_one


def finish(section, returned, updated):
    levels = section.shape[1]

    def at(count, carry):
        for t in range(2):
            span = slice(t * ROWS, (t + 1) * ROWS)

            def level(place):
                return pair(returned[2 * t, place], returned[2 * t + 1, place])

            jump = level(count + 2) - level(count)
            updated[0, count, span] = section[0, count, span] - density_couple * jump
            updated[1, count, span] = section[1, count, span]
            updated[2, count, span] = section[2, count, span]
            updated[3, count, span] = level(count + 1)
            updated[4, count, span] = section[4, count, span] - theta_couple * jump
        return carry

    lax.fori_loop(0, levels, at, 0, unroll=2)


VM = pl.BlockSpec(memory_space=pltpu.VMEM)
SM = pl.BlockSpec(memory_space=pltpu.SMEM)
MESH = pl.DeviceIdType.MESH


def f32(*shape):
    return jax.ShapeDtypeStruct(shape, jnp.float32)


def whole_kernel(
    sizes,
    first,
    second,
    state,
    scale,
    faces,
    flips,
    coupling,
    damping,
    weights,
    section,
    returned,
    tables,
    north_message,
    south_message,
    edges,
    west,
    east,
    before,
    after,
    factors,
    message,
    columns,
    back,
    send_sem,
    recv_sem,
):
    hx, hy, vz = (lax.axis_index(axis) for axis in ("hx", "hy", "vz"))
    size_x, size_y, parts = sizes

    def place(dx=0, dy=0, dz=0):
        return (
            lax.rem(hx + dx + size_x, size_x),
            lax.rem(hy + dy + size_y, size_y),
            lax.rem(vz + dz, parts),
        )

    partners = [place(dx=1), place(dx=-1), place(dy=1), place(dy=-1)]
    partners += [place(dz=d) for d in range(1, parts)]
    barrier = pltpu.get_barrier_semaphore()
    for partner in partners:
        pl.semaphore_signal(barrier, inc=1, device_id=partner, device_id_type=MESH)

    def copy(number, source, target, device):
        return pltpu.make_async_remote_copy(
            src_ref=source,
            dst_ref=target,
            send_sem=send_sem.at[number],
            recv_sem=recv_sem.at[number],
            device_id=device,
            device_id_type=MESH,
        )

    pack_edges(state, edges)
    pl.semaphore_wait(barrier, len(partners))
    to_tables = [
        copy(0, faces, tables.at[0], place(dy=-1)),
        copy(1, flips, tables.at[1], place(dy=-1)),
        copy(2, faces, tables.at[2], place(dy=1)),
        copy(3, flips, tables.at[3], place(dy=1)),
    ]
    for each in to_tables:
        each.start()
    to_edges = [
        copy(4, edges.at[0], after, place(dx=-1)),
        copy(5, edges.at[1], before, place(dx=1)),
    ]
    for each in to_edges:
        each.start()
    for each in to_tables:
        each.wait_recv()
    pack_faces(
        state,
        jnp.concatenate(
            [tables[0, 0:1], tables[1, 0:1], tables[2, 1:2], tables[3, 1:2]], axis=0
        ),
        north_message,
        south_message,
    )
    to_faces = [
        copy(6, north_message, west, place(dy=1)),
        copy(7, south_message, east, place(dy=-1)),
    ]
    for each in to_faces:
        each.start()
    factor(coupling, damping, factors)
    for each in to_edges + to_faces:
        each.wait_recv()
    make_section(
        state,
        scale,
        first,
        second,
        faces[...],
        flips[...],
        west,
        east,
        before[...],
        after[...],
        weights,
        section,
    )
    column_message(section, message)
    to_columns = []
    for d in range(1, parts):
        peer = place(dz=d)
        to_columns.append(copy(7 + d, message.at[peer[2]], columns.at[vz], peer))
        to_columns[-1].start()
    columns[vz] = message[vz]
    for each in to_columns:
        each.wait_recv()
    solve(factors, columns, back)
    to_back = []
    for d in range(1, parts):
        peer = place(dz=d)
        to_back.append(copy(6 + parts + d, back.at[peer[2]], returned.at[vz], peer))
        to_back[-1].start()
    returned[vz] = back[vz]
    for each in to_back:
        each.wait_recv()
    for each in to_tables + to_edges + to_faces + to_columns + to_back:
        each.wait_send()


def per_device(
    sizes,
    prognostic,
    metric,
    first_flux,
    second_flux,
    neighbour_face,
    orientation,
    coupling,
    damping,
):
    levels = prognostic.shape[1]
    parts = sizes[2]
    state = prognostic.reshape(FIELDS, levels, 16, LANES)
    scale = metric.reshape(16, LANES)
    faces = neighbour_face.reshape(4, LANES)
    flips = orientation.reshape(4, LANES)
    couples = coupling.reshape(4, levels * parts, 4, LANES)
    damp = damping.reshape(4, LANES)
    copies = 6 + 2 * parts
    trace = pltpu.VMEM((FIELDS, levels, 4, LANES), jnp.float32)
    column = pltpu.VMEM((parts, levels + 2, 4, LANES), jnp.float32)
    section, returned = pl.pallas_call(
        functools.partial(whole_kernel, sizes),
        out_shape=(f32(FIELDS, levels, 16, LANES), f32(parts, levels + 2, 4, LANES)),
        in_specs=[SM, SM] + [VM] * 7,
        out_specs=(VM, VM),
        scratch_shapes=[
            pltpu.VMEM((4, 4, LANES), jnp.int32),
            trace,
            trace,
            pltpu.VMEM((2, 16, LANES), jnp.float32),
            trace,
            trace,
            pltpu.VMEM((16, LANES), jnp.float32),
            pltpu.VMEM((16, LANES), jnp.float32),
            pltpu.VMEM((5, levels * parts // 2, ROWS, LANES), jnp.float32),
            column,
            column,
            column,
            pltpu.SemaphoreType.DMA((copies,)),
            pltpu.SemaphoreType.DMA((copies,)),
        ],
        compiler_params=pltpu.CompilerParams(collective_id=0, has_side_effects=True),
        name="exchange",
    )(
        first_flux,
        second_flux,
        state,
        scale,
        faces,
        flips,
        couples,
        damp,
        jnp.asarray(weight_table()),
    )
    updated = pl.pallas_call(
        finish,
        out_shape=f32(FIELDS, levels, 16, LANES),
        in_specs=[VM, VM],
        out_specs=VM,
        name="finish",
    )(section, returned)
    return updated.reshape(prognostic.shape)


def solution(mesh):
    placed = (
        P(None, "vz", None, None, "hy", "hx"),
        P(None, None, "hy", "hx"),
        P(),
        P(),
        P(None, "hy", "hx"),
        P(None, "hy", "hx"),
        P(None, None, "vz", None, "hy", "hx"),
        P("vz", None, "hy", "hx"),
    )
    sizes = (mesh.shape["hx"], mesh.shape["hy"], mesh.shape["vz"])
    return jax.shard_map(
        functools.partial(per_device, sizes),
        mesh=mesh,
        in_specs=placed,
        out_specs=P(None, "vz", None, None, "hy", "hx"),
        check_vma=False,
    )
```

```python
import functools

import jax
import jax.numpy as jnp
import numpy as np
from jax import lax
from jax.experimental import pallas as pl
from jax.experimental.pallas import tpu as pltpu
from jax.sharding import PartitionSpec as P

step_size = 0.05
lift_weight = 6.0
gravity_couple = 0.5
density_couple = 0.3
theta_couple = 0.4

FIELDS = 5
ROWS = 8
LANES = 128


def derivative_matrix():
    points = np.array([-1.0, -1.0 / np.sqrt(5.0), 1.0 / np.sqrt(5.0), 1.0])
    number = points.shape[0]
    barycentric = np.ones(number)
    for source in range(number):
        for another in range(number):
            if another != source:
                barycentric[source] = barycentric[source] / (points[source] - points[another])
    matrix = np.zeros((number, number))
    for target in range(number):
        for source in range(number):
            if target != source:
                matrix[target, source] = (
                    barycentric[source] / barycentric[target] / (points[target] - points[source])
                )
        matrix[target, target] = -np.sum(matrix[target])
    return matrix


def weight_table():
    d = derivative_matrix()
    half = 0.5 * lift_weight
    along = np.zeros((7, ROWS))
    for row in range(ROWS):
        i = row % 4
        for offset in range(-3, 4):
            if 0 <= i + offset < 4:
                along[offset + 3, row] = -d[i, i + offset]
    cx = np.array([{0: -half, 3: half}.get(r % 4, 0.0) for r in range(ROWS)])
    along[3] += cx
    across = np.zeros((2, 2, 2, ROWS))
    for tile in range(2):
        for other in range(2):
            for row in range(ROWS):
                jl = row // 4
                j = 2 * tile + jl
                across[tile, other, 0, row] = -d[j, 2 * other + jl]
                across[tile, other, 1, row] = -d[j, 2 * other + 1 - jl]
    cy = np.zeros((2, ROWS))
    cy[0, :4] = -half
    cy[1, 4:] = half
    for tile in range(2):
        across[tile, tile, 0] += cy[tile]
    own = np.zeros((2, ROWS))
    for tile in range(2):
        own[tile] = -np.abs(cx) - np.abs(cy[tile])
    rows = np.concatenate(
        [along, across.reshape(8, ROWS), cx[None], np.abs(cx)[None], cy, np.abs(cy), own]
    )
    return np.ascontiguousarray(
        np.broadcast_to(rows[:, :, None], rows.shape + (LANES,)).astype(np.float32)
    )


def rows_of(shape=(ROWS, LANES)):
    return lax.broadcasted_iota(jnp.int32, shape, 0)


def lanes_of(shape=(ROWS, LANES)):
    return lax.broadcasted_iota(jnp.int32, shape, 1)


def spread(row):
    return jnp.broadcast_to(row, (ROWS, LANES))


def node_rows(face, flip):
    k = rows_of() % 4
    k = jnp.where(flip == 1, 3 - k, k)
    return jnp.where(
        face == 0, 4 * k, jnp.where(face == 1, 4 * k + 3, jnp.where(face == 2, k, 12 + k))
    )


def take_rows(tile, index):
    return jnp.take_along_axis(tile, index, axis=0, mode="promise_in_bounds")


def take_nodes(low, high, node):
    index = jnp.where(node >= ROWS, node - ROWS, node)
    return jnp.where(node >= ROWS, take_rows(high, index), take_rows(low, index))


def halves(low, high):
    return jnp.where(rows_of() < 4, low, high)


def pack_faces(state, tables, north_message, south_message):
    levels = state.shape[1]
    node = halves(
        node_rows(spread(tables[0:1]), spread(tables[1:2])),
        node_rows(spread(tables[2:3]), spread(tables[3:4])),
    )

    def at(count, carry):
        for field in range(FIELDS):
            chosen = take_nodes(
                state[field, count, 0:ROWS], state[field, count, ROWS : 2 * ROWS], node
            )
            north_message[field, count] = chosen[0:4]
            south_message[field, count] = chosen[4:8]
        return carry

    lax.fori_loop(0, levels, at, 0, unroll=2)


def pack_edges(state, edges):
    levels = state.shape[1]
    lane = lanes_of()
    zero = state[0, 0, 0:ROWS] - state[0, 0, 0:ROWS]

    def at(count, held):
        held = list(held)
        for field in range(FIELDS):
            number = field * levels + count
            at_first = lane == number
            at_last = lane == lax.rem(number + LANES - 1, LANES)
            for tile in range(2):
                moved = pltpu.roll(
                    state[field, count, tile * ROWS : (tile + 1) * ROWS], number, 1
                )
                held[tile] = jnp.where(at_first, moved, held[tile])
                held[2 + tile] = jnp.where(at_last, moved, held[2 + tile])
        return tuple(held)

    held = lax.fori_loop(0, levels, at, (zero,) * 4)
    for tile in range(2):
        edges[0, tile * ROWS : (tile + 1) * ROWS] = held[tile]
        edges[1, tile * ROWS : (tile + 1) * ROWS] = held[2 + tile]


def edge_values(before, after, faces, flips):
    def lane_value(table, row, lane):
        return jnp.broadcast_to(table[row : row + 1, lane : lane + 1], (ROWS, LANES))

    from_before = take_nodes(
        before[0:ROWS],
        before[ROWS : 2 * ROWS],
        node_rows(lane_value(faces, 2, 0), lane_value(flips, 2, 0)),
    )
    from_after = take_nodes(
        after[0:ROWS],
        after[ROWS : 2 * ROWS],
        node_rows(lane_value(faces, 3, LANES - 1), lane_value(flips, 3, LANES - 1)),
    )
    return halves(pltpu.roll(from_before, 1, 1), pltpu.roll(from_after, LANES - 1, 1))


def make_section(
    state, scale, first, second, faces, flips, sides, before, after, weights, section, targets
):
    levels = state.shape[1]
    row, lane = rows_of(), lanes_of()
    node = halves(
        node_rows(
            pltpu.roll(spread(faces[2:3]), LANES - 1, 1),
            pltpu.roll(spread(flips[2:3]), LANES - 1, 1),
        ),
        node_rows(pltpu.roll(spread(faces[3:4]), 1, 1), pltpu.roll(spread(flips[3:4]), 1, 1)),
    )
    edge = edge_values(before, after, faces, flips)
    at_edge = ((row < 4) & (lane == 0)) | ((row >= 4) & (lane == LANES - 1))
    place = side_rows()

    def at(count, carry):
        q1 = [[None] * 2 for _ in range(FIELDS)]
        q2 = [[None] * 2 for _ in range(FIELDS)]
        rest = [[None] * 2 for _ in range(FIELDS)]
        own = [[None] * 2 for _ in range(FIELDS)]
        for field in range(FIELDS):
            number = field * levels + count
            tiles = [state[field, count, t * ROWS : (t + 1) * ROWS] for t in range(2)]
            swapped = [pltpu.roll(tile, 4, 0) for tile in tiles]
            chosen = take_nodes(tiles[0], tiles[1], node)
            across = halves(pltpu.roll(chosen, 1, 1), pltpu.roll(chosen, LANES - 1, 1))
            shift = lax.rem(2 * LANES - number, LANES)
            across = jnp.where(at_edge, pltpu.roll(edge, shift, 1), across)
            if sides is not None:
                beside = pair(sides[0][field, count], sides[1][field, count])
            for t in range(2):
                total = weights[3] * tiles[t]
                for offset in (-3, -2, -1, 1, 2, 3):
                    total += weights[offset + 3] * pltpu.roll(tiles[t], (-offset) % ROWS, 0)
                if sides is not None:
                    along = take_rows(beside, place[t])
                    total -= weights[15] * along
                q1[field][t] = total
                total = -weights[17 + t] * across
                for other in range(2):
                    total += weights[7 + 4 * t + 2 * other] * tiles[other]
                    total += weights[8 + 4 * t + 2 * other] * swapped[other]
                q2[field][t] = total
                if field in targets:
                    total = weights[21 + t] * tiles[t] + weights[19 + t] * across
                    if sides is not None:
                        total += weights[16] * along
                    rest[field][t] = total
                    own[field][t] = tiles[t]
        for field in targets:
            for t in range(2):
                total = rest[field][t]
                for other in range(FIELDS):
                    total += first[field, other] * q1[other][t]
                    total += second[field, other] * q2[other][t]
                section[field, count, t * ROWS : (t + 1) * ROWS] = (
                    own[field][t] + step_size * scale[t * ROWS : (t + 1) * ROWS] * total
                )
        return carry

    lax.fori_loop(0, levels, at, 0)


def side_rows():
    row = rows_of()
    left = row % 4 < 2
    return [jnp.where(left, 2 * tile + row // 4, 4 + 2 * tile + row // 4) for tile in range(2)]


def add_sides(scale, first, sides, weights, section, targets):
    levels = section.shape[1]
    place = side_rows()

    def at(count, carry):
        beside = [pair(sides[0][g, count], sides[1][g, count]) for g in range(FIELDS)]
        for t in range(2):
            span = slice(t * ROWS, (t + 1) * ROWS)
            along = [take_rows(each, place[t]) for each in beside]
            for field in targets:
                total = first[field, 0] * along[0]
                for other in range(1, FIELDS):
                    total += first[field, other] * along[other]
                total = weights[16] * along[field] - weights[15] * total
                section[field, count, span] += step_size * scale[span] * total
        return carry

    lax.fori_loop(0, levels, at, 0, unroll=2)


def point_pair(part):
    return (1, 2) if part == 0 else (0, 3)


def gathered(entries, base, part):
    row = rows_of()
    low, high = point_pair(part)
    total = None
    for m in range(4):
        if entries[m] is None:
            continue
        index = jnp.where(row % 2 == 0, base[m] + low, base[m] + high)
        moved = take_rows(entries[m], index)
        total = moved if total is None else jnp.where(row // 2 == m, moved, total)
    for m in range(4):
        if entries[m] is None:
            total = jnp.where(row // 2 == m, 0.0, total)
    return total


def scattered(tile, m):
    return take_rows(tile, 2 * m + (rows_of() % 4) // 2)


def column_message(section, message, part):
    levels = section.shape[1]
    for t in range(2):
        span = slice(t * ROWS, (t + 1) * ROWS)
        warm = [section[4, count, span] for count in range(levels)]
        entries = []
        for count in range(levels):
            total = section[3, count, span]
            if count + 1 < levels:
                total = total - gravity_couple * warm[count + 1]
            if count > 0:
                total = total + gravity_couple * warm[count - 1]
            entries.append(total)
        entries += [warm[0], warm[levels - 1]]
        entries += [None] * (-len(entries) % 4)
        for p in range(len(entries) // 4):
            for side in range(2):
                message[2 * t + side, p] = gathered(
                    entries[4 * p : 4 * p + 4], [4 * side] * 4, part
                )


def pair(low, high):
    return jnp.concatenate([low, high], axis=0)


def factor(coupling, damping, factors):
    levels = coupling.shape[1]
    half = levels // 2
    damp = pair(damping[...], damping[...])
    zero = damp - damp

    def at(t, carry):
        far_ratio, far_second, near_ratio, near_second = carry
        up = levels - 1 - t
        entry_a = pair(coupling[0, t], coupling[3, up])
        entry_b = pair(coupling[1, t], coupling[2, up])
        entry_d = pair(coupling[2, t], coupling[1, up])
        entry_e = pair(coupling[3, t], coupling[0, up])
        centre = entry_a + entry_b + entry_d + entry_e + damp
        reduced = entry_a * far_ratio - entry_b
        pivot = centre + entry_a * far_second - reduced * near_ratio
        inverse = 1.0 / pivot
        ratio = -(entry_d + reduced * near_second) * inverse
        second = -entry_e * inverse
        factors[0, t] = inverse
        factors[1, t] = entry_a * inverse
        factors[2, t] = reduced * inverse
        factors[3, t] = ratio
        factors[4, t] = second
        return near_ratio, near_second, ratio, second

    lax.fori_loop(0, half, at, (zero,) * 4)


def solve(factors, columns, message, part, count):
    parts = columns.shape[0]
    levels = parts * count
    half = levels // 2

    def entry_of(d, place):
        return scattered(columns[d, place // 4], place % 4)

    def source(level):
        d, place = level // count, level % count
        entry = entry_of(d, place)
        if place == 0 and d > 0:
            entry = entry + gravity_couple * entry_of(d - 1, count + 1)
        if place == count - 1 and d < parts - 1:
            entry = entry - gravity_couple * entry_of(d + 1, count)
        return entry

    far = near = jnp.zeros((ROWS, LANES), jnp.float32)
    scaled = []
    for t in range(half):
        entry = halves(source(t), source(levels - 1 - t)) * factors[0, t]
        far, near = near, (entry + factors[1, t] * far) - factors[2, t] * near
        scaled.append(near)
    top, under = half - 1, half - 2
    ratio_1, ratio_2 = factors[3, top], factors[3, under]
    second_1, second_2 = factors[4, top], factors[4, under]
    here = 1.0 - second_1 * pltpu.roll(second_2, 4, 0)
    there = ratio_1 - second_1 * pltpu.roll(ratio_2, 4, 0)
    right = scaled[top] - second_1 * pltpu.roll(scaled[under], 4, 0)
    here_2 = pltpu.roll(here, 4, 0)
    there_2 = pltpu.roll(there, 4, 0)
    right_2 = pltpu.roll(right, 4, 0)
    mine = (right * here_2 - there * right_2) / (here * here_2 - there * there_2)
    next_one, next_two = mine, pltpu.roll(mine, 4, 0)
    found = [None] * half
    found[top] = mine
    for t in range(half - 2, -1, -1):
        found[t] = (scaled[t] - factors[4, t] * next_two) - factors[3, t] * next_one
        next_one, next_two = found[t], next_one
    for d in range(parts):
        for p in range((count + 2 + 3) // 4):
            entries, base = [], []
            for m in range(4):
                level = d * count - 1 + 4 * p + m
                inside = 0 <= level < levels and 4 * p + m < count + 2
                low = level < half
                entries.append((found[level] if low else found[levels - 1 - level]) if inside else None)
                base.append(0 if low else 4)
            message[d, p] = gathered(entries, base, part)


def finish(section, returned, updated):
    levels = section.shape[1]
    point = rows_of() % 4
    inner = (point == 1) | (point == 2)
    for t in range(2):
        span = slice(t * ROWS, (t + 1) * ROWS)

        def level(place):
            p, m = place // 4, place % 4
            both = [
                jnp.where(
                    inner,
                    scattered(returned[0, 2 * t + side, p], m),
                    scattered(returned[1, 2 * t + side, p], m),
                )
                for side in range(2)
            ]
            return halves(both[0], both[1])

        speeds = [level(place) for place in range(levels + 2)]
        for count in range(levels):
            jump = speeds[count + 2] - speeds[count]
            updated[0, count, span] = section[0, count, span] - density_couple * jump
            updated[1, count, span] = section[1, count, span]
            updated[2, count, span] = section[2, count, span]
            updated[3, count, span] = speeds[count + 1]
            updated[4, count, span] = section[4, count, span] - theta_couple * jump


VM = pl.BlockSpec(memory_space=pltpu.VMEM)
SM = pl.BlockSpec(memory_space=pltpu.SMEM)
ANY = pl.BlockSpec(memory_space=pl.ANY)
MESH = pl.DeviceIdType.MESH


def f32(*shape):
    return jax.ShapeDtypeStruct(shape, jnp.float32)


def whole_kernel(
    sizes,
    first,
    second,
    state_in,
    scale,
    faces,
    flips,
    coupling_in,
    damping,
    weights,
    section,
    returned,
    state,
    coupling,
    tables,
    north_message,
    south_message,
    edges,
    west,
    east,
    before,
    after,
    factors,
    message,
    columns,
    back,
    send_sem,
    recv_sem,
    load_sem,
):
    hx, hy, vz = (lax.axis_index(axis) for axis in ("hx", "hy", "vz"))
    size_x, size_y, parts = sizes

    def place(dx=0, dy=0, dz=0):
        return (
            lax.rem(hx + dx + size_x, size_x),
            lax.rem(hy + dy + size_y, size_y),
            lax.rem(vz + dz, parts),
        )

    partners = [place(dx=1), place(dx=-1), place(dy=1), place(dy=-1)]
    partners += [place(dz=d) for d in range(1, parts)]
    barrier = pltpu.get_barrier_semaphore()
    for partner in partners:
        pl.semaphore_signal(barrier, inc=1, device_id=partner, device_id_type=MESH)

    def copy(number, source, target, device):
        return pltpu.make_async_remote_copy(
            src_ref=source,
            dst_ref=target,
            send_sem=send_sem.at[number],
            recv_sem=recv_sem.at[number],
            device_id=device,
            device_id_type=MESH,
        )

    load_state = pltpu.make_async_copy(state_in, state, load_sem.at[0])
    load_coupling = pltpu.make_async_copy(coupling_in, coupling, load_sem.at[1])
    load_state.start()
    load_coupling.start()
    pl.semaphore_wait(barrier, len(partners))
    to_tables = [
        copy(0, faces, tables.at[0], place(dy=-1)),
        copy(1, flips, tables.at[1], place(dy=-1)),
        copy(2, faces, tables.at[2], place(dy=1)),
        copy(3, flips, tables.at[3], place(dy=1)),
    ]
    for each in to_tables:
        each.start()
    load_state.wait()
    pack_edges(state, edges)
    to_edges = [
        copy(4, edges.at[0], after, place(dx=-1)),
        copy(5, edges.at[1], before, place(dx=1)),
    ]
    for each in to_edges:
        each.start()
    for each in to_tables:
        each.wait_recv()
    pack_faces(
        state,
        jnp.concatenate(
            [tables[0, 0:1], tables[1, 0:1], tables[2, 1:2], tables[3, 1:2]], axis=0
        ),
        north_message,
        south_message,
    )
    to_faces = [
        copy(6, north_message, west, place(dy=1)),
        copy(7, south_message, east, place(dy=-1)),
    ]
    for each in to_faces:
        each.start()
    for each in to_edges:
        each.wait_recv()

    def sections(sides, targets):
        make_section(
            state,
            scale,
            first,
            second,
            faces[...],
            flips[...],
            sides,
            before[...],
            after[...],
            weights,
            section,
            targets,
        )

    def spread_out(part, base, source, target):
        sent = []
        for d in range(1, parts):
            peer = place(dz=d)
            number = base + part * (parts - 1) + d - 1
            sent.append(copy(number, source.at[part, peer[2]], target.at[part, vz], peer))
            sent[-1].start()
        target[part, vz] = source[part, vz]
        return sent

    first_out, first_back = 8, 8 + 2 * (parts - 1)
    count = state.shape[1]
    sections(None, (3, 4))
    column_message(section, message.at[0], 0)
    out_0 = spread_out(0, first_out, message, columns)
    for each in to_faces:
        each.wait_recv()
    add_sides(scale, first, (west, east), weights, section, (3, 4))
    column_message(section, message.at[1], 1)
    out_1 = spread_out(1, first_out, message, columns)
    load_coupling.wait()
    factor(coupling, damping, factors)
    for each in out_0:
        each.wait_recv()
    solve(factors, columns.at[0], back.at[0], 0, count)
    back_0 = spread_out(0, first_back, back, returned)
    for each in out_1:
        each.wait_recv()
    solve(factors, columns.at[1], back.at[1], 1, count)
    back_1 = spread_out(1, first_back, back, returned)
    sections((west, east), (0, 1, 2))
    for each in back_0 + back_1:
        each.wait_recv()
    for each in to_tables + to_edges + to_faces + out_0 + out_1 + back_0 + back_1:
        each.wait_send()


def per_device(
    sizes,
    prognostic,
    metric,
    first_flux,
    second_flux,
    neighbour_face,
    orientation,
    coupling,
    damping,
):
    levels = prognostic.shape[1]
    parts = sizes[2]
    state = prognostic.reshape(FIELDS, levels, 16, LANES)
    scale = metric.reshape(16, LANES)
    faces = neighbour_face.reshape(4, LANES)
    flips = orientation.reshape(4, LANES)
    couples = coupling.reshape(4, levels * parts, 4, LANES)
    damp = damping.reshape(4, LANES)
    copies = 8 + 4 * (parts - 1)
    tiles = (levels + 2 + 3) // 4
    trace = pltpu.VMEM((FIELDS, levels, 4, LANES), jnp.float32)
    column = pltpu.VMEM((2, parts, tiles, ROWS, LANES), jnp.float32)
    section, returned = pl.pallas_call(
        functools.partial(whole_kernel, sizes),
        out_shape=(f32(FIELDS, levels, 16, LANES), f32(2, parts, tiles, ROWS, LANES)),
        in_specs=[SM, SM, ANY, VM, VM, VM, ANY, VM, VM],
        out_specs=(VM, VM),
        scratch_shapes=[
            pltpu.VMEM((FIELDS, levels, 16, LANES), jnp.float32),
            pltpu.VMEM((4, levels * parts, 4, LANES), jnp.float32),
            pltpu.VMEM((4, 4, LANES), jnp.int32),
            trace,
            trace,
            pltpu.VMEM((2, 16, LANES), jnp.float32),
            trace,
            trace,
            pltpu.VMEM((16, LANES), jnp.float32),
            pltpu.VMEM((16, LANES), jnp.float32),
            pltpu.VMEM((5, levels * parts // 2, ROWS, LANES), jnp.float32),
            column,
            column,
            column,
            pltpu.SemaphoreType.DMA((copies,)),
            pltpu.SemaphoreType.DMA((copies,)),
            pltpu.SemaphoreType.DMA((2,)),
        ],
        compiler_params=pltpu.CompilerParams(collective_id=0, has_side_effects=True),
        name="exchange",
    )(
        first_flux,
        second_flux,
        state,
        scale,
        faces,
        flips,
        couples,
        damp,
        jnp.asarray(weight_table()),
    )
    updated = pl.pallas_call(
        finish,
        out_shape=f32(FIELDS, levels, 16, LANES),
        in_specs=[VM, VM],
        out_specs=VM,
        name="finish",
    )(section, returned)
    return updated.reshape(prognostic.shape)


def solution(mesh):
    placed = (
        P(None, "vz", None, None, "hy", "hx"),
        P(None, None, "hy", "hx"),
        P(),
        P(),
        P(None, "hy", "hx"),
        P(None, "hy", "hx"),
        P(None, None, "vz", None, "hy", "hx"),
        P("vz", None, "hy", "hx"),
    )
    sizes = (mesh.shape["hx"], mesh.shape["hy"], mesh.shape["vz"])
    return jax.shard_map(
        functools.partial(per_device, sizes),
        mesh=mesh,
        in_specs=placed,
        out_specs=P(None, "vz", None, None, "hy", "hx"),
        check_vma=False,
    )
```

```python
import functools

import jax
import jax.numpy as jnp
import numpy as np
from jax import lax
from jax.experimental import pallas as pl
from jax.experimental.pallas import tpu as pltpu
from jax.sharding import PartitionSpec as P

step_size = 0.05
lift_weight = 6.0
gravity_couple = 0.5
density_couple = 0.3
theta_couple = 0.4

FIELDS = 5
ROWS = 8
LANES = 128


def derivative_matrix():
    points = np.array([-1.0, -1.0 / np.sqrt(5.0), 1.0 / np.sqrt(5.0), 1.0])
    number = points.shape[0]
    barycentric = np.ones(number)
    for source in range(number):
        for another in range(number):
            if another != source:
                barycentric[source] = barycentric[source] / (points[source] - points[another])
    matrix = np.zeros((number, number))
    for target in range(number):
        for source in range(number):
            if target != source:
                matrix[target, source] = (
                    barycentric[source] / barycentric[target] / (points[target] - points[source])
                )
        matrix[target, target] = -np.sum(matrix[target])
    return matrix


def weight_table():
    d = derivative_matrix()
    half = 0.5 * lift_weight
    along = np.zeros((7, ROWS))
    for row in range(ROWS):
        i = row % 4
        for offset in range(-3, 4):
            if 0 <= i + offset < 4:
                along[offset + 3, row] = -d[i, i + offset]
    cx = np.array([{0: -half, 3: half}.get(r % 4, 0.0) for r in range(ROWS)])
    along[3] += cx
    across = np.zeros((2, 2, 2, ROWS))
    for tile in range(2):
        for other in range(2):
            for row in range(ROWS):
                jl = row // 4
                j = 2 * tile + jl
                across[tile, other, 0, row] = -d[j, 2 * other + jl]
                across[tile, other, 1, row] = -d[j, 2 * other + 1 - jl]
    cy = np.zeros((2, ROWS))
    cy[0, :4] = -half
    cy[1, 4:] = half
    for tile in range(2):
        across[tile, tile, 0] += cy[tile]
    own = np.zeros((2, ROWS))
    for tile in range(2):
        own[tile] = -np.abs(cx) - np.abs(cy[tile])
    rows = np.concatenate(
        [along, across.reshape(8, ROWS), cx[None], np.abs(cx)[None], cy, np.abs(cy), own]
    )
    return np.ascontiguousarray(
        np.broadcast_to(rows[:, :, None], rows.shape + (LANES,)).astype(np.float32)
    )


def rows_of(shape=(ROWS, LANES)):
    return lax.broadcasted_iota(jnp.int32, shape, 0)


def lanes_of(shape=(ROWS, LANES)):
    return lax.broadcasted_iota(jnp.int32, shape, 1)


def spread(row):
    return jnp.broadcast_to(row, (ROWS, LANES))


def node_rows(face, flip):
    k = rows_of() % 4
    k = jnp.where(flip == 1, 3 - k, k)
    return jnp.where(
        face == 0, 4 * k, jnp.where(face == 1, 4 * k + 3, jnp.where(face == 2, k, 12 + k))
    )


def take_rows(tile, index):
    return jnp.take_along_axis(tile, index, axis=0, mode="promise_in_bounds")


def take_nodes(low, high, node):
    index = jnp.where(node >= ROWS, node - ROWS, node)
    return jnp.where(node >= ROWS, take_rows(high, index), take_rows(low, index))


def halves(low, high):
    return jnp.where(rows_of() < 4, low, high)


def pack_faces(state, tables, north_message, south_message):
    levels = state.shape[1]
    node = halves(
        node_rows(spread(tables[0:1]), spread(tables[1:2])),
        node_rows(spread(tables[2:3]), spread(tables[3:4])),
    )

    def at(count, carry):
        for field in range(FIELDS):
            chosen = take_nodes(
                state[field, count, 0:ROWS], state[field, count, ROWS : 2 * ROWS], node
            )
            north_message[field, count] = chosen[0:4]
            south_message[field, count] = chosen[4:8]
        return carry

    lax.fori_loop(0, levels, at, 0, unroll=2)


def pack_edges(state, edges):
    levels = state.shape[1]
    lane = lanes_of()
    zero = state[0, 0, 0:ROWS] - state[0, 0, 0:ROWS]

    def at(count, held):
        held = list(held)
        for field in range(FIELDS):
            number = field * levels + count
            at_first = lane == number
            at_last = lane == lax.rem(number + LANES - 1, LANES)
            for tile in range(2):
                moved = pltpu.roll(
                    state[field, count, tile * ROWS : (tile + 1) * ROWS], number, 1
                )
                held[tile] = jnp.where(at_first, moved, held[tile])
                held[2 + tile] = jnp.where(at_last, moved, held[2 + tile])
        return tuple(held)

    held = lax.fori_loop(0, levels, at, (zero,) * 4)
    for tile in range(2):
        edges[0, tile * ROWS : (tile + 1) * ROWS] = held[tile]
        edges[1, tile * ROWS : (tile + 1) * ROWS] = held[2 + tile]


def edge_values(before, after, faces, flips):
    def lane_value(table, row, lane):
        return jnp.broadcast_to(table[row : row + 1, lane : lane + 1], (ROWS, LANES))

    from_before = take_nodes(
        before[0:ROWS],
        before[ROWS : 2 * ROWS],
        node_rows(lane_value(faces, 2, 0), lane_value(flips, 2, 0)),
    )
    from_after = take_nodes(
        after[0:ROWS],
        after[ROWS : 2 * ROWS],
        node_rows(lane_value(faces, 3, LANES - 1), lane_value(flips, 3, LANES - 1)),
    )
    return halves(pltpu.roll(from_before, 1, 1), pltpu.roll(from_after, LANES - 1, 1))


def make_section(
    state, scale, first, second, faces, flips, sides, before, after, weights, section, targets
):
    levels = state.shape[1]
    node = halves(
        node_rows(
            pltpu.roll(spread(faces[2:3]), LANES - 1, 1),
            pltpu.roll(spread(flips[2:3]), LANES - 1, 1),
        ),
        node_rows(pltpu.roll(spread(faces[3:4]), 1, 1), pltpu.roll(spread(flips[3:4]), 1, 1)),
    )
    edge = None if before is None else edge_values(before, after, faces, flips)
    at_edge = edge_mask()
    place = side_rows()

    def at(count, carry):
        q1 = [[None] * 2 for _ in range(FIELDS)]
        q2 = [[None] * 2 for _ in range(FIELDS)]
        rest = [[None] * 2 for _ in range(FIELDS)]
        own = [[None] * 2 for _ in range(FIELDS)]
        for field in range(FIELDS):
            number = field * levels + count
            tiles = [state[field, count, t * ROWS : (t + 1) * ROWS] for t in range(2)]
            swapped = [pltpu.roll(tile, 4, 0) for tile in tiles]
            chosen = take_nodes(tiles[0], tiles[1], node)
            across = halves(pltpu.roll(chosen, 1, 1), pltpu.roll(chosen, LANES - 1, 1))
            if edge is None:
                across = jnp.where(at_edge, 0.0, across)
            else:
                across = jnp.where(at_edge, edge_level(edge, number), across)
            if sides is not None:
                beside = pair(sides[0][field, count], sides[1][field, count])
            for t in range(2):
                total = weights[3] * tiles[t]
                for offset in (-3, -2, -1, 1, 2, 3):
                    total += weights[offset + 3] * pltpu.roll(tiles[t], (-offset) % ROWS, 0)
                if sides is not None:
                    along = take_rows(beside, place[t])
                    total -= weights[15] * along
                q1[field][t] = total
                total = -weights[17 + t] * across
                for other in range(2):
                    total += weights[7 + 4 * t + 2 * other] * tiles[other]
                    total += weights[8 + 4 * t + 2 * other] * swapped[other]
                q2[field][t] = total
                if field in targets:
                    total = weights[21 + t] * tiles[t] + weights[19 + t] * across
                    if sides is not None:
                        total += weights[16] * along
                    rest[field][t] = total
                    own[field][t] = tiles[t]
        for field in targets:
            for t in range(2):
                total = rest[field][t]
                for other in range(FIELDS):
                    total += first[field, other] * q1[other][t]
                    total += second[field, other] * q2[other][t]
                section[field, count, t * ROWS : (t + 1) * ROWS] = (
                    own[field][t] + step_size * scale[t * ROWS : (t + 1) * ROWS] * total
                )
        return carry

    lax.fori_loop(0, levels, at, 0)


def edge_mask():
    row, lane = rows_of(), lanes_of()
    return ((row < 4) & (lane == 0)) | ((row >= 4) & (lane == LANES - 1))


def edge_level(edge, number):
    return pltpu.roll(edge, lax.rem(2 * LANES - number, LANES), 1)


def add_edges(scale, second, faces, flips, before, after, weights, section, targets):
    levels = section.shape[1]
    edge = edge_values(before, after, faces, flips)
    at_edge = edge_mask()

    def at(count, carry):
        across = [
            jnp.where(at_edge, edge_level(edge, g * levels + count), 0.0) for g in range(FIELDS)
        ]
        for field in targets:
            total = second[field, 0] * across[0]
            for other in range(1, FIELDS):
                total += second[field, other] * across[other]
            for t in range(2):
                span = slice(t * ROWS, (t + 1) * ROWS)
                change = weights[19 + t] * across[field] - weights[17 + t] * total
                section[field, count, span] += step_size * scale[span] * change
        return carry

    lax.fori_loop(0, levels, at, 0, unroll=2)


def side_rows():
    row = rows_of()
    left = row % 4 < 2
    return [jnp.where(left, 2 * tile + row // 4, 4 + 2 * tile + row // 4) for tile in range(2)]


def add_sides(scale, first, sides, weights, section, targets):
    levels = section.shape[1]
    place = side_rows()

    def at(count, carry):
        beside = [pair(sides[0][g, count], sides[1][g, count]) for g in range(FIELDS)]
        for t in range(2):
            span = slice(t * ROWS, (t + 1) * ROWS)
            along = [take_rows(each, place[t]) for each in beside]
            for field in targets:
                total = first[field, 0] * along[0]
                for other in range(1, FIELDS):
                    total += first[field, other] * along[other]
                total = weights[16] * along[field] - weights[15] * total
                section[field, count, span] += step_size * scale[span] * total
        return carry

    lax.fori_loop(0, levels, at, 0, unroll=2)


def point_pair(part):
    return (1, 2) if part == 0 else (0, 3)


def gathered(entries, base, part):
    row = rows_of()
    low, high = point_pair(part)
    total = None
    for m in range(4):
        if entries[m] is None:
            continue
        index = jnp.where(row % 2 == 0, base[m] + low, base[m] + high)
        moved = take_rows(entries[m], index)
        total = moved if total is None else jnp.where(row // 2 == m, moved, total)
    for m in range(4):
        if entries[m] is None:
            total = jnp.where(row // 2 == m, 0.0, total)
    return total


def put_tile(message, p, tile):
    for half in range(2):
        if 2 * p + half < message.shape[0]:
            message[2 * p + half] = tile[4 * half : 4 * half + 4]


def scattered(message, place):
    tile = message[place // 2]
    return take_rows(pair(tile, tile), 2 * (place % 2) + (rows_of() % 4) // 2)


def column_message(section, message, part):
    levels = section.shape[1]
    for t in range(2):
        span = slice(t * ROWS, (t + 1) * ROWS)
        warm = [section[4, count, span] for count in range(levels)]
        entries = []
        for count in range(levels):
            total = section[3, count, span]
            if count + 1 < levels:
                total = total - gravity_couple * warm[count + 1]
            if count > 0:
                total = total + gravity_couple * warm[count - 1]
            entries.append(total)
        entries += [warm[0], warm[levels - 1]]
        entries += [None] * (-len(entries) % 4)
        for p in range(len(entries) // 4):
            for side in range(2):
                tile = gathered(entries[4 * p : 4 * p + 4], [4 * side] * 4, part)
                put_tile(message.at[2 * t + side], p, tile)


def pair(low, high):
    return jnp.concatenate([low, high], axis=0)


def factor(coupling, damping, factors):
    levels = coupling.shape[1]
    half = levels // 2
    damp = pair(damping[...], damping[...])
    zero = damp - damp

    def at(t, carry):
        far_ratio, far_second, near_ratio, near_second = carry
        up = levels - 1 - t
        entry_a = pair(coupling[0, t], coupling[3, up])
        entry_b = pair(coupling[1, t], coupling[2, up])
        entry_d = pair(coupling[2, t], coupling[1, up])
        entry_e = pair(coupling[3, t], coupling[0, up])
        centre = entry_a + entry_b + entry_d + entry_e + damp
        reduced = entry_a * far_ratio - entry_b
        pivot = centre + entry_a * far_second - reduced * near_ratio
        inverse = 1.0 / pivot
        ratio = -(entry_d + reduced * near_second) * inverse
        second = -entry_e * inverse
        factors[0, t] = inverse
        factors[1, t] = entry_a * inverse
        factors[2, t] = reduced * inverse
        factors[3, t] = ratio
        factors[4, t] = second
        return near_ratio, near_second, ratio, second

    lax.fori_loop(0, half, at, (zero,) * 4)


def solve(factors, columns, message, part, count):
    parts = columns.shape[0]
    levels = parts * count
    half = levels // 2

    def entry_of(d, place):
        return scattered(columns.at[d], place)

    def source(level):
        d, place = level // count, level % count
        entry = entry_of(d, place)
        if place == 0 and d > 0:
            entry = entry + gravity_couple * entry_of(d - 1, count + 1)
        if place == count - 1 and d < parts - 1:
            entry = entry - gravity_couple * entry_of(d + 1, count)
        return entry

    far = near = jnp.zeros((ROWS, LANES), jnp.float32)
    scaled = []
    for t in range(half):
        entry = halves(source(t), source(levels - 1 - t)) * factors[0, t]
        far, near = near, (entry + factors[1, t] * far) - factors[2, t] * near
        scaled.append(near)
    top, under = half - 1, half - 2
    ratio_1, ratio_2 = factors[3, top], factors[3, under]
    second_1, second_2 = factors[4, top], factors[4, under]
    here = 1.0 - second_1 * pltpu.roll(second_2, 4, 0)
    there = ratio_1 - second_1 * pltpu.roll(ratio_2, 4, 0)
    right = scaled[top] - second_1 * pltpu.roll(scaled[under], 4, 0)
    here_2 = pltpu.roll(here, 4, 0)
    there_2 = pltpu.roll(there, 4, 0)
    right_2 = pltpu.roll(right, 4, 0)
    mine = (right * here_2 - there * right_2) / (here * here_2 - there * there_2)
    next_one, next_two = mine, pltpu.roll(mine, 4, 0)
    found = [None] * half
    found[top] = mine
    for t in range(half - 2, -1, -1):
        found[t] = (scaled[t] - factors[4, t] * next_two) - factors[3, t] * next_one
        next_one, next_two = found[t], next_one
    for d in range(parts):
        for p in range((count + 2 + 3) // 4):
            entries, base = [], []
            for m in range(4):
                level = d * count - 1 + 4 * p + m
                inside = 0 <= level < levels and 4 * p + m < count + 2
                low = level < half
                entries.append((found[level] if low else found[levels - 1 - level]) if inside else None)
                base.append(0 if low else 4)
            put_tile(message.at[d], p, gathered(entries, base, part))


def finish(section, returned, updated):
    levels = section.shape[1]
    point = rows_of() % 4
    inner = (point == 1) | (point == 2)
    for t in range(2):
        span = slice(t * ROWS, (t + 1) * ROWS)

        def level(place):
            both = [
                jnp.where(
                    inner,
                    scattered(returned.at[0, 2 * t + side], place),
                    scattered(returned.at[1, 2 * t + side], place),
                )
                for side in range(2)
            ]
            return halves(both[0], both[1])

        speeds = [level(place) for place in range(levels + 2)]
        for count in range(levels):
            jump = speeds[count + 2] - speeds[count]
            updated[0, count, span] = section[0, count, span] - density_couple * jump
            updated[1, count, span] = section[1, count, span]
            updated[2, count, span] = section[2, count, span]
            updated[3, count, span] = speeds[count + 1]
            updated[4, count, span] = section[4, count, span] - theta_couple * jump


VM = pl.BlockSpec(memory_space=pltpu.VMEM)
SM = pl.BlockSpec(memory_space=pltpu.SMEM)
ANY = pl.BlockSpec(memory_space=pl.ANY)
MESH = pl.DeviceIdType.MESH


def f32(*shape):
    return jax.ShapeDtypeStruct(shape, jnp.float32)


def whole_kernel(
    sizes,
    first,
    second,
    state_in,
    scale,
    faces,
    flips,
    coupling_in,
    damping,
    weights,
    section,
    returned,
    state,
    coupling,
    tables,
    north_message,
    south_message,
    edges,
    west,
    east,
    before,
    after,
    factors,
    message,
    columns,
    back,
    send_sem,
    recv_sem,
    load_sem,
):
    hx, hy, vz = (lax.axis_index(axis) for axis in ("hx", "hy", "vz"))
    size_x, size_y, parts = sizes

    def place(dx=0, dy=0, dz=0):
        return (
            lax.rem(hx + dx + size_x, size_x),
            lax.rem(hy + dy + size_y, size_y),
            lax.rem(vz + dz, parts),
        )

    partners = [place(dx=1), place(dx=-1), place(dy=1), place(dy=-1)]
    partners += [place(dz=d) for d in range(1, parts)]
    barrier = pltpu.get_barrier_semaphore()
    for partner in partners:
        pl.semaphore_signal(barrier, inc=1, device_id=partner, device_id_type=MESH)

    def copy(number, source, target, device):
        return pltpu.make_async_remote_copy(
            src_ref=source,
            dst_ref=target,
            send_sem=send_sem.at[number],
            recv_sem=recv_sem.at[number],
            device_id=device,
            device_id_type=MESH,
        )

    load_state = pltpu.make_async_copy(state_in, state, load_sem.at[0])
    load_coupling = pltpu.make_async_copy(coupling_in, coupling, load_sem.at[1])
    load_state.start()
    load_coupling.start()

    def sections(sides, edge_pair, targets):
        make_section(
            state,
            scale,
            first,
            second,
            faces[...],
            flips[...],
            sides,
            edge_pair[0],
            edge_pair[1],
            weights,
            section,
            targets,
        )

    load_state.wait()
    pack_edges(state, edges)
    pl.semaphore_wait(barrier, len(partners))
    to_edges = [
        copy(4, edges.at[0], after, place(dx=-1)),
        copy(5, edges.at[1], before, place(dx=1)),
    ]
    to_tables = [
        copy(0, faces, tables.at[0], place(dy=-1)),
        copy(1, flips, tables.at[1], place(dy=-1)),
        copy(2, faces, tables.at[2], place(dy=1)),
        copy(3, flips, tables.at[3], place(dy=1)),
    ]
    for each in to_edges + to_tables:
        each.start()
    sections(None, (None, None), (3, 4))
    for each in to_tables:
        each.wait_recv()
    pack_faces(
        state,
        jnp.concatenate(
            [tables[0, 0:1], tables[1, 0:1], tables[2, 1:2], tables[3, 1:2]], axis=0
        ),
        north_message,
        south_message,
    )
    to_faces = [
        copy(6, north_message, west, place(dy=1)),
        copy(7, south_message, east, place(dy=-1)),
    ]
    for each in to_faces:
        each.start()

    def spread_out(part, base, source, target):
        sent = []
        for d in range(1, parts):
            peer = place(dz=d)
            number = base + part * (parts - 1) + d - 1
            sent.append(copy(number, source.at[part, peer[2]], target.at[part, vz], peer))
            sent[-1].start()
        target[part, vz] = source[part, vz]
        return sent

    first_out, first_back = 8, 8 + 2 * (parts - 1)
    count = state.shape[1]
    for each in to_edges:
        each.wait_recv()
    add_edges(
        scale, second, faces[...], flips[...], before[...], after[...], weights, section, (3, 4)
    )
    column_message(section, message.at[0], 0)
    out_0 = spread_out(0, first_out, message, columns)
    for each in to_faces:
        each.wait_recv()
    add_sides(scale, first, (west, east), weights, section, (3, 4))
    column_message(section, message.at[1], 1)
    out_1 = spread_out(1, first_out, message, columns)
    load_coupling.wait()
    factor(coupling, damping, factors)
    for each in out_0:
        each.wait_recv()
    solve(factors, columns.at[0], back.at[0], 0, count)
    back_0 = spread_out(0, first_back, back, returned)
    for each in out_1:
        each.wait_recv()
    solve(factors, columns.at[1], back.at[1], 1, count)
    back_1 = spread_out(1, first_back, back, returned)
    sections((west, east), (before[...], after[...]), (0, 1, 2))
    for each in back_0 + back_1:
        each.wait_recv()
    for each in to_tables + to_edges + to_faces + out_0 + out_1 + back_0 + back_1:
        each.wait_send()


def per_device(
    sizes,
    prognostic,
    metric,
    first_flux,
    second_flux,
    neighbour_face,
    orientation,
    coupling,
    damping,
):
    levels = prognostic.shape[1]
    parts = sizes[2]
    state = prognostic.reshape(FIELDS, levels, 16, LANES)
    scale = metric.reshape(16, LANES)
    faces = neighbour_face.reshape(4, LANES)
    flips = orientation.reshape(4, LANES)
    couples = coupling.reshape(4, levels * parts, 4, LANES)
    damp = damping.reshape(4, LANES)
    copies = 8 + 4 * (parts - 1)
    tiles = (levels + 3) // 2
    trace = pltpu.VMEM((FIELDS, levels, 4, LANES), jnp.float32)
    column = pltpu.VMEM((2, parts, tiles, 4, LANES), jnp.float32)
    section, returned = pl.pallas_call(
        functools.partial(whole_kernel, sizes),
        out_shape=(f32(FIELDS, levels, 16, LANES), f32(2, parts, tiles, 4, LANES)),
        in_specs=[SM, SM, ANY, VM, VM, VM, ANY, VM, VM],
        out_specs=(VM, VM),
        scratch_shapes=[
            pltpu.VMEM((FIELDS, levels, 16, LANES), jnp.float32),
            pltpu.VMEM((4, levels * parts, 4, LANES), jnp.float32),
            pltpu.VMEM((4, 4, LANES), jnp.int32),
            trace,
            trace,
            pltpu.VMEM((2, 16, LANES), jnp.float32),
            trace,
            trace,
            pltpu.VMEM((16, LANES), jnp.float32),
            pltpu.VMEM((16, LANES), jnp.float32),
            pltpu.VMEM((5, levels * parts // 2, ROWS, LANES), jnp.float32),
            column,
            column,
            column,
            pltpu.SemaphoreType.DMA((copies,)),
            pltpu.SemaphoreType.DMA((copies,)),
            pltpu.SemaphoreType.DMA((2,)),
        ],
        compiler_params=pltpu.CompilerParams(collective_id=0, has_side_effects=True),
        name="exchange",
    )(
        first_flux,
        second_flux,
        state,
        scale,
        faces,
        flips,
        couples,
        damp,
        jnp.asarray(weight_table()),
    )
    updated = pl.pallas_call(
        finish,
        out_shape=f32(FIELDS, levels, 16, LANES),
        in_specs=[VM, VM],
        out_specs=VM,
        name="finish",
    )(section, returned)
    return updated.reshape(prognostic.shape)


def solution(mesh):
    placed = (
        P(None, "vz", None, None, "hy", "hx"),
        P(None, None, "hy", "hx"),
        P(),
        P(),
        P(None, "hy", "hx"),
        P(None, "hy", "hx"),
        P(None, None, "vz", None, "hy", "hx"),
        P("vz", None, "hy", "hx"),
    )
    sizes = (mesh.shape["hx"], mesh.shape["hy"], mesh.shape["vz"])
    return jax.shard_map(
        functools.partial(per_device, sizes),
        mesh=mesh,
        in_specs=placed,
        out_specs=P(None, "vz", None, None, "hy", "hx"),
        check_vma=False,
    )
```

```python
import functools

import jax
import jax.numpy as jnp
import numpy as np
from jax import lax
from jax.experimental import pallas as pl
from jax.experimental.pallas import tpu as pltpu
from jax.sharding import PartitionSpec as P

step_size = 0.05
lift_weight = 6.0
gravity_couple = 0.5
density_couple = 0.3
theta_couple = 0.4

FIELDS = 5
ROWS = 8
LANES = 128


def derivative_matrix():
    points = np.array([-1.0, -1.0 / np.sqrt(5.0), 1.0 / np.sqrt(5.0), 1.0])
    number = points.shape[0]
    barycentric = np.ones(number)
    for source in range(number):
        for another in range(number):
            if another != source:
                barycentric[source] = barycentric[source] / (points[source] - points[another])
    matrix = np.zeros((number, number))
    for target in range(number):
        for source in range(number):
            if target != source:
                matrix[target, source] = (
                    barycentric[source] / barycentric[target] / (points[target] - points[source])
                )
        matrix[target, target] = -np.sum(matrix[target])
    return matrix


def weight_table():
    d = derivative_matrix()
    half = 0.5 * lift_weight
    along = np.zeros((7, ROWS))
    for row in range(ROWS):
        i = row % 4
        for offset in range(-3, 4):
            if 0 <= i + offset < 4:
                along[offset + 3, row] = -d[i, i + offset]
    cx = np.array([{0: -half, 3: half}.get(r % 4, 0.0) for r in range(ROWS)])
    along[3] += cx
    across = np.zeros((2, 2, 2, ROWS))
    for tile in range(2):
        for other in range(2):
            for row in range(ROWS):
                jl = row // 4
                j = 2 * tile + jl
                across[tile, other, 0, row] = -d[j, 2 * other + jl]
                across[tile, other, 1, row] = -d[j, 2 * other + 1 - jl]
    cy = np.zeros((2, ROWS))
    cy[0, :4] = -half
    cy[1, 4:] = half
    for tile in range(2):
        across[tile, tile, 0] += cy[tile]
    own = np.zeros((2, ROWS))
    for tile in range(2):
        own[tile] = -np.abs(cx) - np.abs(cy[tile])
    rows = np.concatenate(
        [along, across.reshape(8, ROWS), cx[None], np.abs(cx)[None], cy, np.abs(cy), own]
    )
    return np.ascontiguousarray(
        np.broadcast_to(rows[:, :, None], rows.shape + (LANES,)).astype(np.float32)
    )


def rows_of(shape=(ROWS, LANES)):
    return lax.broadcasted_iota(jnp.int32, shape, 0)


def lanes_of(shape=(ROWS, LANES)):
    return lax.broadcasted_iota(jnp.int32, shape, 1)


def spread(row):
    return jnp.broadcast_to(row, (ROWS, LANES))


def node_rows(face, flip):
    k = rows_of() % 4
    k = jnp.where(flip == 1, 3 - k, k)
    return jnp.where(
        face == 0, 4 * k, jnp.where(face == 1, 4 * k + 3, jnp.where(face == 2, k, 12 + k))
    )


def take_rows(tile, index):
    return jnp.take_along_axis(tile, index, axis=0, mode="promise_in_bounds")


def take_nodes(low, high, node):
    index = jnp.where(node >= ROWS, node - ROWS, node)
    return jnp.where(node >= ROWS, take_rows(high, index), take_rows(low, index))


def halves(low, high):
    return jnp.where(rows_of() < 4, low, high)


def pack_faces(state, tables, north_message, south_message):
    levels = state.shape[1]
    node = halves(
        node_rows(spread(tables[0:1]), spread(tables[1:2])),
        node_rows(spread(tables[2:3]), spread(tables[3:4])),
    )

    def at(count, carry):
        for field in range(FIELDS):
            chosen = take_nodes(
                state[field, count, 0:ROWS], state[field, count, ROWS : 2 * ROWS], node
            )
            north_message[field, count] = chosen[0:4]
            south_message[field, count] = chosen[4:8]
        return carry

    lax.fori_loop(0, levels, at, 0, unroll=2)


def pack_edges(state, edges):
    levels = state.shape[1]
    lane = lanes_of()
    zero = state[0, 0, 0:ROWS] - state[0, 0, 0:ROWS]

    def at(count, held):
        held = list(held)
        for field in range(FIELDS):
            number = field * levels + count
            at_first = lane == number
            at_last = lane == lax.rem(number + LANES - 1, LANES)
            for tile in range(2):
                moved = pltpu.roll(
                    state[field, count, tile * ROWS : (tile + 1) * ROWS], number, 1
                )
                held[tile] = jnp.where(at_first, moved, held[tile])
                held[2 + tile] = jnp.where(at_last, moved, held[2 + tile])
        return tuple(held)

    held = lax.fori_loop(0, levels, at, (zero,) * 4)
    for tile in range(2):
        edges[0, tile * ROWS : (tile + 1) * ROWS] = held[tile]
        edges[1, tile * ROWS : (tile + 1) * ROWS] = held[2 + tile]


def edge_values(before, after, faces, flips):
    def lane_value(table, row, lane):
        return jnp.broadcast_to(table[row : row + 1, lane : lane + 1], (ROWS, LANES))

    from_before = take_nodes(
        before[0:ROWS],
        before[ROWS : 2 * ROWS],
        node_rows(lane_value(faces, 2, 0), lane_value(flips, 2, 0)),
    )
    from_after = take_nodes(
        after[0:ROWS],
        after[ROWS : 2 * ROWS],
        node_rows(lane_value(faces, 3, LANES - 1), lane_value(flips, 3, LANES - 1)),
    )
    return halves(pltpu.roll(from_before, 1, 1), pltpu.roll(from_after, LANES - 1, 1))


def make_section(
    state, scale, first, second, faces, flips, sides, before, after, weights, section, targets
):
    levels = state.shape[1]
    node = halves(
        node_rows(
            pltpu.roll(spread(faces[2:3]), LANES - 1, 1),
            pltpu.roll(spread(flips[2:3]), LANES - 1, 1),
        ),
        node_rows(pltpu.roll(spread(faces[3:4]), 1, 1), pltpu.roll(spread(flips[3:4]), 1, 1)),
    )
    edge = None if before is None else edge_values(before, after, faces, flips)
    at_edge = edge_mask()
    place = side_rows()

    def at(count, carry):
        q1 = [[None] * 2 for _ in range(FIELDS)]
        q2 = [[None] * 2 for _ in range(FIELDS)]
        rest = [[None] * 2 for _ in range(FIELDS)]
        own = [[None] * 2 for _ in range(FIELDS)]
        for field in range(FIELDS):
            number = field * levels + count
            tiles = [state[field, count, t * ROWS : (t + 1) * ROWS] for t in range(2)]
            swapped = [pltpu.roll(tile, 4, 0) for tile in tiles]
            chosen = take_nodes(tiles[0], tiles[1], node)
            across = halves(pltpu.roll(chosen, 1, 1), pltpu.roll(chosen, LANES - 1, 1))
            if edge is None:
                across = jnp.where(at_edge, 0.0, across)
            else:
                across = jnp.where(at_edge, edge_level(edge, number), across)
            if sides is not None:
                beside = pair(sides[0][field, count], sides[1][field, count])
            for t in range(2):
                total = weights[3] * tiles[t]
                for offset in (-3, -2, -1, 1, 2, 3):
                    total += weights[offset + 3] * pltpu.roll(tiles[t], (-offset) % ROWS, 0)
                if sides is not None:
                    along = take_rows(beside, place[t])
                    total -= weights[15] * along
                q1[field][t] = total
                total = -weights[17 + t] * across
                for other in range(2):
                    total += weights[7 + 4 * t + 2 * other] * tiles[other]
                    total += weights[8 + 4 * t + 2 * other] * swapped[other]
                q2[field][t] = total
                if field in targets:
                    total = weights[21 + t] * tiles[t] + weights[19 + t] * across
                    if sides is not None:
                        total += weights[16] * along
                    rest[field][t] = total
                    own[field][t] = tiles[t]
        for field in targets:
            for t in range(2):
                total = rest[field][t]
                for other in range(FIELDS):
                    total += first[field, other] * q1[other][t]
                    total += second[field, other] * q2[other][t]
                section[field, count, t * ROWS : (t + 1) * ROWS] = (
                    own[field][t] + step_size * scale[t * ROWS : (t + 1) * ROWS] * total
                )
        return carry

    lax.fori_loop(0, levels, at, 0)


def edge_mask():
    row, lane = rows_of(), lanes_of()
    return ((row < 4) & (lane == 0)) | ((row >= 4) & (lane == LANES - 1))


def edge_level(edge, number):
    return pltpu.roll(edge, lax.rem(2 * LANES - number, LANES), 1)


def add_edges(scale, second, faces, flips, before, after, weights, section, targets):
    levels = section.shape[1]
    edge = edge_values(before, after, faces, flips)
    at_edge = edge_mask()

    def at(count, carry):
        across = [
            jnp.where(at_edge, edge_level(edge, g * levels + count), 0.0) for g in range(FIELDS)
        ]
        for field in targets:
            total = second[field, 0] * across[0]
            for other in range(1, FIELDS):
                total += second[field, other] * across[other]
            for t in range(2):
                span = slice(t * ROWS, (t + 1) * ROWS)
                change = weights[19 + t] * across[field] - weights[17 + t] * total
                section[field, count, span] += step_size * scale[span] * change
        return carry

    lax.fori_loop(0, levels, at, 0, unroll=2)


def side_rows():
    row = rows_of()
    left = row % 4 < 2
    return [jnp.where(left, 2 * tile + row // 4, 4 + 2 * tile + row // 4) for tile in range(2)]


def add_sides(scale, first, sides, weights, section, targets):
    levels = section.shape[1]
    place = side_rows()

    def at(count, carry):
        beside = [pair(sides[0][g, count], sides[1][g, count]) for g in range(FIELDS)]
        for t in range(2):
            span = slice(t * ROWS, (t + 1) * ROWS)
            along = [take_rows(each, place[t]) for each in beside]
            for field in targets:
                total = first[field, 0] * along[0]
                for other in range(1, FIELDS):
                    total += first[field, other] * along[other]
                total = weights[16] * along[field] - weights[15] * total
                section[field, count, span] += step_size * scale[span] * total
        return carry

    lax.fori_loop(0, levels, at, 0, unroll=2)


def point_pair(part):
    return (1, 2) if part == 0 else (0, 3)


def gathered(entries, base, part):
    row = rows_of()
    low, high = point_pair(part)
    total = None
    for m in range(4):
        if entries[m] is None:
            continue
        index = jnp.where(row % 2 == 0, base[m] + low, base[m] + high)
        moved = take_rows(entries[m], index)
        total = moved if total is None else jnp.where(row // 2 == m, moved, total)
    for m in range(4):
        if entries[m] is None:
            total = jnp.where(row // 2 == m, 0.0, total)
    return total


def put_tile(message, p, tile):
    for half in range(2):
        if 2 * p + half < message.shape[0]:
            message[2 * p + half] = tile[4 * half : 4 * half + 4]


def scattered(message, place):
    tile = message[place // 2]
    return take_rows(pair(tile, tile), 2 * (place % 2) + (rows_of() % 4) // 2)


def column_message(section, message, part, only_edges=False):
    levels = section.shape[1]
    lane = lanes_of()
    for t in range(2):
        span = slice(t * ROWS, (t + 1) * ROWS)
        warm = [section[4, count, span] for count in range(levels)]
        entries = []
        for count in range(levels):
            total = section[3, count, span]
            if count + 1 < levels:
                total = total - gravity_couple * warm[count + 1]
            if count > 0:
                total = total + gravity_couple * warm[count - 1]
            entries.append(total)
        entries += [warm[0], warm[levels - 1]]
        entries += [None] * (-len(entries) % 4)
        for side in range(2):
            packed = None
            for p in range(len(entries) // 4):
                tile = gathered(entries[4 * p : 4 * p + 4], [4 * side] * 4, part)
                if only_edges:
                    moved = pltpu.roll(tile, p + t, 1) if p + t else tile
                    packed = moved if p == 0 else jnp.where(lane == p, moved, packed)
                else:
                    put_tile(message.at[2 * t + side], p, tile)
            if only_edges:
                message[2 * t + side] = packed


def replace_edges(columns, patches, j):
    lane = lanes_of((4, LANES))
    target = (j // 2) * (LANES - 1)
    for d in range(columns.shape[0]):
        for p in range((columns.shape[1] + 1) // 2):
            moved = pltpu.roll(patches[d], lax.rem(target + LANES - p, LANES), 1)
            for half in range(2):
                if 2 * p + half < columns.shape[1]:
                    columns[d, 2 * p + half] = jnp.where(
                        lane == target, moved[4 * half : 4 * half + 4], columns[d, 2 * p + half]
                    )


def pair(low, high):
    return jnp.concatenate([low, high], axis=0)


def factor(coupling, damping, factors):
    levels = coupling.shape[1]
    half = levels // 2
    damp = pair(damping[...], damping[...])
    zero = damp - damp

    def at(t, carry):
        far_ratio, far_second, near_ratio, near_second = carry
        up = levels - 1 - t
        entry_a = pair(coupling[0, t], coupling[3, up])
        entry_b = pair(coupling[1, t], coupling[2, up])
        entry_d = pair(coupling[2, t], coupling[1, up])
        entry_e = pair(coupling[3, t], coupling[0, up])
        centre = entry_a + entry_b + entry_d + entry_e + damp
        reduced = entry_a * far_ratio - entry_b
        pivot = centre + entry_a * far_second - reduced * near_ratio
        inverse = 1.0 / pivot
        ratio = -(entry_d + reduced * near_second) * inverse
        second = -entry_e * inverse
        factors[0, t] = inverse
        factors[1, t] = entry_a * inverse
        factors[2, t] = reduced * inverse
        factors[3, t] = ratio
        factors[4, t] = second
        return near_ratio, near_second, ratio, second

    lax.fori_loop(0, half, at, (zero,) * 4)


def solve(factors, columns, message, part, count):
    parts = columns.shape[0]
    levels = parts * count
    half = levels // 2

    def entry_of(d, place):
        return scattered(columns.at[d], place)

    def source(level):
        d, place = level // count, level % count
        entry = entry_of(d, place)
        if place == 0 and d > 0:
            entry = entry + gravity_couple * entry_of(d - 1, count + 1)
        if place == count - 1 and d < parts - 1:
            entry = entry - gravity_couple * entry_of(d + 1, count)
        return entry

    far = near = jnp.zeros((ROWS, LANES), jnp.float32)
    scaled = []
    for t in range(half):
        entry = halves(source(t), source(levels - 1 - t)) * factors[0, t]
        far, near = near, (entry + factors[1, t] * far) - factors[2, t] * near
        scaled.append(near)
    top, under = half - 1, half - 2
    ratio_1, ratio_2 = factors[3, top], factors[3, under]
    second_1, second_2 = factors[4, top], factors[4, under]
    here = 1.0 - second_1 * pltpu.roll(second_2, 4, 0)
    there = ratio_1 - second_1 * pltpu.roll(ratio_2, 4, 0)
    right = scaled[top] - second_1 * pltpu.roll(scaled[under], 4, 0)
    here_2 = pltpu.roll(here, 4, 0)
    there_2 = pltpu.roll(there, 4, 0)
    right_2 = pltpu.roll(right, 4, 0)
    mine = (right * here_2 - there * right_2) / (here * here_2 - there * there_2)
    next_one, next_two = mine, pltpu.roll(mine, 4, 0)
    found = [None] * half
    found[top] = mine
    for t in range(half - 2, -1, -1):
        found[t] = (scaled[t] - factors[4, t] * next_two) - factors[3, t] * next_one
        next_one, next_two = found[t], next_one
    for d in range(parts):
        for p in range((count + 2 + 3) // 4):
            entries, base = [], []
            for m in range(4):
                level = d * count - 1 + 4 * p + m
                inside = 0 <= level < levels and 4 * p + m < count + 2
                low = level < half
                entries.append((found[level] if low else found[levels - 1 - level]) if inside else None)
                base.append(0 if low else 4)
            put_tile(message.at[d], p, gathered(entries, base, part))


def finish(section, returned, updated):
    levels = section.shape[1]
    point = rows_of() % 4
    inner = (point == 1) | (point == 2)
    for t in range(2):
        span = slice(t * ROWS, (t + 1) * ROWS)

        def level(place):
            both = [
                jnp.where(
                    inner,
                    scattered(returned.at[0, 2 * t + side], place),
                    scattered(returned.at[1, 2 * t + side], place),
                )
                for side in range(2)
            ]
            return halves(both[0], both[1])

        speeds = [level(place) for place in range(levels + 2)]
        for count in range(levels):
            jump = speeds[count + 2] - speeds[count]
            updated[0, count, span] = section[0, count, span] - density_couple * jump
            updated[1, count, span] = section[1, count, span]
            updated[2, count, span] = section[2, count, span]
            updated[3, count, span] = speeds[count + 1]
            updated[4, count, span] = section[4, count, span] - theta_couple * jump


VM = pl.BlockSpec(memory_space=pltpu.VMEM)
SM = pl.BlockSpec(memory_space=pltpu.SMEM)
ANY = pl.BlockSpec(memory_space=pl.ANY)
MESH = pl.DeviceIdType.MESH


def f32(*shape):
    return jax.ShapeDtypeStruct(shape, jnp.float32)


def whole_kernel(
    sizes,
    first,
    second,
    state_in,
    scale,
    faces,
    flips,
    coupling_in,
    damping,
    weights,
    section,
    returned,
    state,
    coupling,
    tables,
    north_message,
    south_message,
    edges,
    west,
    east,
    before,
    after,
    factors,
    message,
    columns,
    back,
    patch,
    patches,
    send_sem,
    recv_sem,
    load_sem,
):
    hx, hy, vz = (lax.axis_index(axis) for axis in ("hx", "hy", "vz"))
    size_x, size_y, parts = sizes

    def place(dx=0, dy=0, dz=0):
        return (
            lax.rem(hx + dx + size_x, size_x),
            lax.rem(hy + dy + size_y, size_y),
            lax.rem(vz + dz, parts),
        )

    partners = [place(dx=1), place(dx=-1), place(dy=1), place(dy=-1)]
    partners += [place(dz=d) for d in range(1, parts)]
    barrier = pltpu.get_barrier_semaphore()
    for partner in partners:
        pl.semaphore_signal(barrier, inc=1, device_id=partner, device_id_type=MESH)

    def copy(number, source, target, device):
        return pltpu.make_async_remote_copy(
            src_ref=source,
            dst_ref=target,
            send_sem=send_sem.at[number],
            recv_sem=recv_sem.at[number],
            device_id=device,
            device_id_type=MESH,
        )

    load_state = pltpu.make_async_copy(state_in, state, load_sem.at[0])
    load_coupling = pltpu.make_async_copy(coupling_in, coupling, load_sem.at[1])
    load_state.start()
    load_coupling.start()

    def sections(sides, edge_pair, targets):
        make_section(
            state,
            scale,
            first,
            second,
            faces[...],
            flips[...],
            sides,
            edge_pair[0],
            edge_pair[1],
            weights,
            section,
            targets,
        )

    load_state.wait()
    pack_edges(state, edges)
    pl.semaphore_wait(barrier, len(partners))
    to_edges = [
        copy(4, edges.at[0], after, place(dx=-1)),
        copy(5, edges.at[1], before, place(dx=1)),
    ]
    to_tables = [
        copy(0, faces, tables.at[0], place(dy=-1)),
        copy(1, flips, tables.at[1], place(dy=-1)),
        copy(2, faces, tables.at[2], place(dy=1)),
        copy(3, flips, tables.at[3], place(dy=1)),
    ]
    for each in to_edges + to_tables:
        each.start()
    def spread_out(part, base, source, target):
        sent = []
        for d in range(1, parts):
            peer = place(dz=d)
            number = base + part * (parts - 1) + d - 1
            sent.append(copy(number, source.at[part, peer[2]], target.at[part, vz], peer))
            sent[-1].start()
        target[part, vz] = source[part, vz]
        return sent

    first_out, first_back = 8, 8 + 2 * (parts - 1)
    count = state.shape[1]
    sections(None, (None, None), (3, 4))
    column_message(section, message.at[0], 0)
    out_0 = spread_out(0, first_out, message, columns)
    for each in to_tables:
        each.wait_recv()
    pack_faces(
        state,
        jnp.concatenate(
            [tables[0, 0:1], tables[1, 0:1], tables[2, 1:2], tables[3, 1:2]], axis=0
        ),
        north_message,
        south_message,
    )
    to_faces = [
        copy(6, north_message, west, place(dy=1)),
        copy(7, south_message, east, place(dy=-1)),
    ]
    for each in to_faces:
        each.start()
    load_coupling.wait()
    factor(coupling, damping, factors)
    for each in to_edges:
        each.wait_recv()
    add_edges(
        scale, second, faces[...], flips[...], before[...], after[...], weights, section, (3, 4)
    )
    column_message(section, patch, 0, only_edges=True)
    to_patches = []
    for d in range(1, parts):
        peer = place(dz=d)
        number = 8 + 4 * (parts - 1) + d - 1
        to_patches.append(copy(number, patch.at[peer[2]], patches.at[vz], peer))
        to_patches[-1].start()
    patches[vz] = patch[vz]
    for each in to_faces:
        each.wait_recv()
    add_sides(scale, first, (west, east), weights, section, (3, 4))
    column_message(section, message.at[1], 1)
    out_1 = spread_out(1, first_out, message, columns)
    for each in out_0 + to_patches:
        each.wait_recv()
    replace_edges(columns.at[0], patches, vz)
    solve(factors, columns.at[0], back.at[0], 0, count)
    back_0 = spread_out(0, first_back, back, returned)
    for each in out_1:
        each.wait_recv()
    solve(factors, columns.at[1], back.at[1], 1, count)
    back_1 = spread_out(1, first_back, back, returned)
    sections((west, east), (before[...], after[...]), (0, 1, 2))
    for each in back_0 + back_1:
        each.wait_recv()
    sent = to_tables + to_edges + to_faces + to_patches + out_0 + out_1 + back_0 + back_1
    for each in sent:
        each.wait_send()


def per_device(
    sizes,
    prognostic,
    metric,
    first_flux,
    second_flux,
    neighbour_face,
    orientation,
    coupling,
    damping,
):
    levels = prognostic.shape[1]
    parts = sizes[2]
    state = prognostic.reshape(FIELDS, levels, 16, LANES)
    scale = metric.reshape(16, LANES)
    faces = neighbour_face.reshape(4, LANES)
    flips = orientation.reshape(4, LANES)
    couples = coupling.reshape(4, levels * parts, 4, LANES)
    damp = damping.reshape(4, LANES)
    copies = 8 + 5 * (parts - 1)
    lanes_out = pltpu.VMEM((parts, ROWS, LANES), jnp.float32)
    tiles = (levels + 3) // 2
    trace = pltpu.VMEM((FIELDS, levels, 4, LANES), jnp.float32)
    column = pltpu.VMEM((2, parts, tiles, 4, LANES), jnp.float32)
    section, returned = pl.pallas_call(
        functools.partial(whole_kernel, sizes),
        out_shape=(f32(FIELDS, levels, 16, LANES), f32(2, parts, tiles, 4, LANES)),
        in_specs=[SM, SM, ANY, VM, VM, VM, ANY, VM, VM],
        out_specs=(VM, VM),
        scratch_shapes=[
            pltpu.VMEM((FIELDS, levels, 16, LANES), jnp.float32),
            pltpu.VMEM((4, levels * parts, 4, LANES), jnp.float32),
            pltpu.VMEM((4, 4, LANES), jnp.int32),
            trace,
            trace,
            pltpu.VMEM((2, 16, LANES), jnp.float32),
            trace,
            trace,
            pltpu.VMEM((16, LANES), jnp.float32),
            pltpu.VMEM((16, LANES), jnp.float32),
            pltpu.VMEM((5, levels * parts // 2, ROWS, LANES), jnp.float32),
            column,
            column,
            column,
            lanes_out,
            lanes_out,
            pltpu.SemaphoreType.DMA((copies,)),
            pltpu.SemaphoreType.DMA((copies,)),
            pltpu.SemaphoreType.DMA((2,)),
        ],
        compiler_params=pltpu.CompilerParams(collective_id=0, has_side_effects=True),
        name="exchange",
    )(
        first_flux,
        second_flux,
        state,
        scale,
        faces,
        flips,
        couples,
        damp,
        jnp.asarray(weight_table()),
    )
    updated = pl.pallas_call(
        finish,
        out_shape=f32(FIELDS, levels, 16, LANES),
        in_specs=[VM, VM],
        out_specs=VM,
        name="finish",
    )(section, returned)
    return updated.reshape(prognostic.shape)


def solution(mesh):
    placed = (
        P(None, "vz", None, None, "hy", "hx"),
        P(None, None, "hy", "hx"),
        P(),
        P(),
        P(None, "hy", "hx"),
        P(None, "hy", "hx"),
        P(None, None, "vz", None, "hy", "hx"),
        P("vz", None, "hy", "hx"),
    )
    sizes = (mesh.shape["hx"], mesh.shape["hy"], mesh.shape["vz"])
    return jax.shard_map(
        functools.partial(per_device, sizes),
        mesh=mesh,
        in_specs=placed,
        out_specs=P(None, "vz", None, None, "hy", "hx"),
        check_vma=False,
    )
```

```python
import functools

import jax
import jax.numpy as jnp
import numpy as np
from jax import lax
from jax.experimental import pallas as pl
from jax.experimental.pallas import tpu as pltpu
from jax.sharding import PartitionSpec as P

step_size = 0.05
lift_weight = 6.0
gravity_couple = 0.5
density_couple = 0.3
theta_couple = 0.4

FIELDS = 5
ROWS = 8
LANES = 128


def derivative_matrix():
    points = np.array([-1.0, -1.0 / np.sqrt(5.0), 1.0 / np.sqrt(5.0), 1.0])
    number = points.shape[0]
    barycentric = np.ones(number)
    for source in range(number):
        for another in range(number):
            if another != source:
                barycentric[source] = barycentric[source] / (points[source] - points[another])
    matrix = np.zeros((number, number))
    for target in range(number):
        for source in range(number):
            if target != source:
                matrix[target, source] = (
                    barycentric[source] / barycentric[target] / (points[target] - points[source])
                )
        matrix[target, target] = -np.sum(matrix[target])
    return matrix


def weight_table():
    d = derivative_matrix()
    half = 0.5 * lift_weight
    along = np.zeros((7, ROWS))
    for row in range(ROWS):
        i = row % 4
        for offset in range(-3, 4):
            if 0 <= i + offset < 4:
                along[offset + 3, row] = -d[i, i + offset]
    cx = np.array([{0: -half, 3: half}.get(r % 4, 0.0) for r in range(ROWS)])
    along[3] += cx
    across = np.zeros((2, 2, 2, ROWS))
    for tile in range(2):
        for other in range(2):
            for row in range(ROWS):
                jl = row // 4
                j = 2 * tile + jl
                across[tile, other, 0, row] = -d[j, 2 * other + jl]
                across[tile, other, 1, row] = -d[j, 2 * other + 1 - jl]
    cy = np.zeros((2, ROWS))
    cy[0, :4] = -half
    cy[1, 4:] = half
    for tile in range(2):
        across[tile, tile, 0] += cy[tile]
    own = np.zeros((2, ROWS))
    for tile in range(2):
        own[tile] = -np.abs(cx) - np.abs(cy[tile])
    rows = np.concatenate(
        [along, across.reshape(8, ROWS), cx[None], np.abs(cx)[None], cy, np.abs(cy), own]
    )
    return np.ascontiguousarray(
        np.broadcast_to(rows[:, :, None], rows.shape + (LANES,)).astype(np.float32)
    )


def rows_of(shape=(ROWS, LANES)):
    return lax.broadcasted_iota(jnp.int32, shape, 0)


def lanes_of(shape=(ROWS, LANES)):
    return lax.broadcasted_iota(jnp.int32, shape, 1)


def spread(row):
    return jnp.broadcast_to(row, (ROWS, LANES))


def node_rows(face, flip):
    k = rows_of() % 4
    k = jnp.where(flip == 1, 3 - k, k)
    return jnp.where(
        face == 0, 4 * k, jnp.where(face == 1, 4 * k + 3, jnp.where(face == 2, k, 12 + k))
    )


def take_rows(tile, index):
    return jnp.take_along_axis(tile, index, axis=0, mode="promise_in_bounds")


def take_nodes(low, high, node):
    index = jnp.where(node >= ROWS, node - ROWS, node)
    return jnp.where(node >= ROWS, take_rows(high, index), take_rows(low, index))


def halves(low, high):
    return jnp.where(rows_of() < 4, low, high)


def pack_faces(state, tables, north_message, south_message):
    levels = state.shape[1]
    node = halves(
        node_rows(spread(tables[0:1]), spread(tables[1:2])),
        node_rows(spread(tables[2:3]), spread(tables[3:4])),
    )

    def at(count, carry):
        for field in range(FIELDS):
            chosen = take_nodes(
                state[field, count, 0:ROWS], state[field, count, ROWS : 2 * ROWS], node
            )
            north_message[field, count] = chosen[0:4]
            south_message[field, count] = chosen[4:8]
        return carry

    lax.fori_loop(0, levels, at, 0, unroll=4)


def pack_edges(state, edges):
    levels = state.shape[1]
    lane = lanes_of()
    zero = state[0, 0, 0:ROWS] - state[0, 0, 0:ROWS]

    def at(count, held):
        held = list(held)
        for field in range(FIELDS):
            number = field * levels + count
            at_first = lane == number
            at_last = lane == lax.rem(number + LANES - 1, LANES)
            for tile in range(2):
                moved = pltpu.roll(
                    state[field, count, tile * ROWS : (tile + 1) * ROWS], number, 1
                )
                held[tile] = jnp.where(at_first, moved, held[tile])
                held[2 + tile] = jnp.where(at_last, moved, held[2 + tile])
        return tuple(held)

    held = lax.fori_loop(0, levels, at, (zero,) * 4, unroll=5)
    for tile in range(2):
        edges[0, tile * ROWS : (tile + 1) * ROWS] = held[tile]
        edges[1, tile * ROWS : (tile + 1) * ROWS] = held[2 + tile]


def edge_values(before, after, faces, flips):
    def lane_value(table, row, lane):
        return jnp.broadcast_to(table[row : row + 1, lane : lane + 1], (ROWS, LANES))

    from_before = take_nodes(
        before[0:ROWS],
        before[ROWS : 2 * ROWS],
        node_rows(lane_value(faces, 2, 0), lane_value(flips, 2, 0)),
    )
    from_after = take_nodes(
        after[0:ROWS],
        after[ROWS : 2 * ROWS],
        node_rows(lane_value(faces, 3, LANES - 1), lane_value(flips, 3, LANES - 1)),
    )
    return halves(pltpu.roll(from_before, 1, 1), pltpu.roll(from_after, LANES - 1, 1))


def make_section(
    state, scale, first, second, faces, flips, sides, before, after, weights, section, targets
):
    levels = state.shape[1]
    node = halves(
        node_rows(
            pltpu.roll(spread(faces[2:3]), LANES - 1, 1),
            pltpu.roll(spread(flips[2:3]), LANES - 1, 1),
        ),
        node_rows(pltpu.roll(spread(faces[3:4]), 1, 1), pltpu.roll(spread(flips[3:4]), 1, 1)),
    )
    edge = None if before is None else edge_values(before, after, faces, flips)
    at_edge = edge_mask()
    place = side_rows()

    def at(count, carry):
        q1 = [[None] * 2 for _ in range(FIELDS)]
        q2 = [[None] * 2 for _ in range(FIELDS)]
        rest = [[None] * 2 for _ in range(FIELDS)]
        own = [[None] * 2 for _ in range(FIELDS)]
        for field in range(FIELDS):
            number = field * levels + count
            tiles = [state[field, count, t * ROWS : (t + 1) * ROWS] for t in range(2)]
            swapped = [pltpu.roll(tile, 4, 0) for tile in tiles]
            chosen = take_nodes(tiles[0], tiles[1], node)
            across = halves(pltpu.roll(chosen, 1, 1), pltpu.roll(chosen, LANES - 1, 1))
            if edge is None:
                across = jnp.where(at_edge, 0.0, across)
            else:
                across = jnp.where(at_edge, edge_level(edge, number), across)
            if sides is not None:
                beside = pair(sides[0][field, count], sides[1][field, count])
            for t in range(2):
                total = weights[3] * tiles[t]
                for offset in (-3, -2, -1, 1, 2, 3):
                    total += weights[offset + 3] * pltpu.roll(tiles[t], (-offset) % ROWS, 0)
                if sides is not None:
                    along = take_rows(beside, place[t])
                    total -= weights[15] * along
                q1[field][t] = total
                total = -weights[17 + t] * across
                for other in range(2):
                    total += weights[7 + 4 * t + 2 * other] * tiles[other]
                    total += weights[8 + 4 * t + 2 * other] * swapped[other]
                q2[field][t] = total
                if field in targets:
                    total = weights[21 + t] * tiles[t] + weights[19 + t] * across
                    if sides is not None:
                        total += weights[16] * along
                    rest[field][t] = total
                    own[field][t] = tiles[t]
        for field in targets:
            for t in range(2):
                total = rest[field][t]
                for other in range(FIELDS):
                    total += first[field, other] * q1[other][t]
                    total += second[field, other] * q2[other][t]
                section[field, count, t * ROWS : (t + 1) * ROWS] = (
                    own[field][t] + step_size * scale[t * ROWS : (t + 1) * ROWS] * total
                )
        return carry

    lax.fori_loop(0, levels, at, 0, unroll=4)


def edge_mask():
    row, lane = rows_of(), lanes_of()
    return ((row < 4) & (lane == 0)) | ((row >= 4) & (lane == LANES - 1))


def edge_level(edge, number):
    return pltpu.roll(edge, lax.rem(2 * LANES - number, LANES), 1)


def add_edges(scale, second, faces, flips, before, after, weights, section, targets):
    levels = section.shape[1]
    edge = edge_values(before, after, faces, flips)
    at_edge = edge_mask()

    def at(count, carry):
        across = [
            jnp.where(at_edge, edge_level(edge, g * levels + count), 0.0) for g in range(FIELDS)
        ]
        for field in targets:
            total = second[field, 0] * across[0]
            for other in range(1, FIELDS):
                total += second[field, other] * across[other]
            for t in range(2):
                span = slice(t * ROWS, (t + 1) * ROWS)
                change = weights[19 + t] * across[field] - weights[17 + t] * total
                section[field, count, span] += step_size * scale[span] * change
        return carry

    lax.fori_loop(0, levels, at, 0, unroll=4)


def side_rows():
    row = rows_of()
    left = row % 4 < 2
    return [jnp.where(left, 2 * tile + row // 4, 4 + 2 * tile + row // 4) for tile in range(2)]


def add_sides(scale, first, sides, weights, section, targets):
    levels = section.shape[1]
    place = side_rows()

    def at(count, carry):
        beside = [pair(sides[0][g, count], sides[1][g, count]) for g in range(FIELDS)]
        for t in range(2):
            span = slice(t * ROWS, (t + 1) * ROWS)
            along = [take_rows(each, place[t]) for each in beside]
            for field in targets:
                total = first[field, 0] * along[0]
                for other in range(1, FIELDS):
                    total += first[field, other] * along[other]
                total = weights[16] * along[field] - weights[15] * total
                section[field, count, span] += step_size * scale[span] * total
        return carry

    lax.fori_loop(0, levels, at, 0, unroll=4)


def point_pair(part):
    return (1, 2) if part == 0 else (0, 3)


def gathered(entries, base, part):
    row = rows_of()
    low, high = point_pair(part)
    total = None
    for m in range(4):
        if entries[m] is None:
            continue
        index = jnp.where(row % 2 == 0, base[m] + low, base[m] + high)
        moved = take_rows(entries[m], index)
        total = moved if total is None else jnp.where(row // 2 == m, moved, total)
    for m in range(4):
        if entries[m] is None:
            total = jnp.where(row // 2 == m, 0.0, total)
    return total


def put_tile(message, p, tile):
    for half in range(2):
        if 2 * p + half < message.shape[0]:
            message[2 * p + half] = tile[4 * half : 4 * half + 4]


def scattered(message, place):
    tile = message[place // 2]
    return take_rows(pair(tile, tile), 2 * (place % 2) + (rows_of() % 4) // 2)


def column_message(section, message, part, only_edges=False):
    levels = section.shape[1]
    lane = lanes_of()
    for t in range(2):
        span = slice(t * ROWS, (t + 1) * ROWS)
        warm = [section[4, count, span] for count in range(levels)]
        entries = []
        for count in range(levels):
            total = section[3, count, span]
            if count + 1 < levels:
                total = total - gravity_couple * warm[count + 1]
            if count > 0:
                total = total + gravity_couple * warm[count - 1]
            entries.append(total)
        entries += [warm[0], warm[levels - 1]]
        entries += [None] * (-len(entries) % 4)
        for side in range(2):
            packed = None
            for p in range(len(entries) // 4):
                tile = gathered(entries[4 * p : 4 * p + 4], [4 * side] * 4, part)
                if only_edges:
                    moved = pltpu.roll(tile, p + t, 1) if p + t else tile
                    packed = moved if p == 0 else jnp.where(lane == p, moved, packed)
                else:
                    put_tile(message.at[2 * t + side], p, tile)
            if only_edges:
                message[2 * t + side] = packed


def replace_edges(columns, patches, j):
    lane = lanes_of((4, LANES))
    target = (j // 2) * (LANES - 1)
    for d in range(columns.shape[0]):
        for p in range((columns.shape[1] + 1) // 2):
            moved = pltpu.roll(patches[d], lax.rem(target + LANES - p, LANES), 1)
            for half in range(2):
                if 2 * p + half < columns.shape[1]:
                    columns[d, 2 * p + half] = jnp.where(
                        lane == target, moved[4 * half : 4 * half + 4], columns[d, 2 * p + half]
                    )


def pair(low, high):
    return jnp.concatenate([low, high], axis=0)


def factor(coupling, damping, factors):
    levels = coupling.shape[1]
    half = levels // 2
    damp = pair(damping[...], damping[...])
    zero = damp - damp

    def at(t, carry):
        far_ratio, far_second, near_ratio, near_second = carry
        up = levels - 1 - t
        entry_a = pair(coupling[0, t], coupling[3, up])
        entry_b = pair(coupling[1, t], coupling[2, up])
        entry_d = pair(coupling[2, t], coupling[1, up])
        entry_e = pair(coupling[3, t], coupling[0, up])
        centre = entry_a + entry_b + entry_d + entry_e + damp
        reduced = entry_a * far_ratio - entry_b
        pivot = centre + entry_a * far_second - reduced * near_ratio
        inverse = 1.0 / pivot
        ratio = -(entry_d + reduced * near_second) * inverse
        second = -entry_e * inverse
        factors[0, t] = inverse
        factors[1, t] = entry_a * inverse
        factors[2, t] = reduced * inverse
        factors[3, t] = ratio
        factors[4, t] = second
        return near_ratio, near_second, ratio, second

    lax.fori_loop(0, half, at, (zero,) * 4)


def solve(factors, columns, message, part, count):
    parts = columns.shape[0]
    levels = parts * count
    half = levels // 2

    def entry_of(d, place):
        return scattered(columns.at[d], place)

    def source(level):
        d, place = level // count, level % count
        entry = entry_of(d, place)
        if place == 0 and d > 0:
            entry = entry + gravity_couple * entry_of(d - 1, count + 1)
        if place == count - 1 and d < parts - 1:
            entry = entry - gravity_couple * entry_of(d + 1, count)
        return entry

    far = near = jnp.zeros((ROWS, LANES), jnp.float32)
    scaled = []
    for t in range(half):
        entry = halves(source(t), source(levels - 1 - t)) * factors[0, t]
        far, near = near, (entry + factors[1, t] * far) - factors[2, t] * near
        scaled.append(near)
    top, under = half - 1, half - 2
    ratio_1, ratio_2 = factors[3, top], factors[3, under]
    second_1, second_2 = factors[4, top], factors[4, under]
    here = 1.0 - second_1 * pltpu.roll(second_2, 4, 0)
    there = ratio_1 - second_1 * pltpu.roll(ratio_2, 4, 0)
    right = scaled[top] - second_1 * pltpu.roll(scaled[under], 4, 0)
    here_2 = pltpu.roll(here, 4, 0)
    there_2 = pltpu.roll(there, 4, 0)
    right_2 = pltpu.roll(right, 4, 0)
    mine = (right * here_2 - there * right_2) / (here * here_2 - there * there_2)
    next_one, next_two = mine, pltpu.roll(mine, 4, 0)
    found = [None] * half
    found[top] = mine
    for t in range(half - 2, -1, -1):
        found[t] = (scaled[t] - factors[4, t] * next_two) - factors[3, t] * next_one
        next_one, next_two = found[t], next_one
    for d in range(parts):
        for p in range((count + 2 + 3) // 4):
            entries, base = [], []
            for m in range(4):
                level = d * count - 1 + 4 * p + m
                inside = 0 <= level < levels and 4 * p + m < count + 2
                low = level < half
                entries.append((found[level] if low else found[levels - 1 - level]) if inside else None)
                base.append(0 if low else 4)
            put_tile(message.at[d], p, gathered(entries, base, part))


def finish(section, returned, updated):
    levels = section.shape[1]
    point = rows_of() % 4
    inner = (point == 1) | (point == 2)
    for t in range(2):
        span = slice(t * ROWS, (t + 1) * ROWS)

        def level(place):
            both = [
                jnp.where(
                    inner,
                    scattered(returned.at[0, 2 * t + side], place),
                    scattered(returned.at[1, 2 * t + side], place),
                )
                for side in range(2)
            ]
            return halves(both[0], both[1])

        speeds = [level(place) for place in range(levels + 2)]
        for count in range(levels):
            jump = speeds[count + 2] - speeds[count]
            updated[0, count, span] = section[0, count, span] - density_couple * jump
            updated[1, count, span] = section[1, count, span]
            updated[2, count, span] = section[2, count, span]
            updated[3, count, span] = speeds[count + 1]
            updated[4, count, span] = section[4, count, span] - theta_couple * jump


VM = pl.BlockSpec(memory_space=pltpu.VMEM)
SM = pl.BlockSpec(memory_space=pltpu.SMEM)
ANY = pl.BlockSpec(memory_space=pl.ANY)
MESH = pl.DeviceIdType.MESH


def f32(*shape):
    return jax.ShapeDtypeStruct(shape, jnp.float32)


def whole_kernel(
    sizes,
    first,
    second,
    state_in,
    scale,
    faces,
    flips,
    coupling_in,
    damping,
    weights,
    section,
    returned,
    state,
    coupling,
    tables,
    north_message,
    south_message,
    edges,
    west,
    east,
    before,
    after,
    factors,
    message,
    columns,
    back,
    patch,
    patches,
    send_sem,
    recv_sem,
    load_sem,
):
    hx, hy, vz = (lax.axis_index(axis) for axis in ("hx", "hy", "vz"))
    size_x, size_y, parts = sizes

    def place(dx=0, dy=0, dz=0):
        return (
            lax.rem(hx + dx + size_x, size_x),
            lax.rem(hy + dy + size_y, size_y),
            lax.rem(vz + dz, parts),
        )

    partners = [place(dx=1), place(dx=-1), place(dy=1), place(dy=-1)]
    partners += [place(dz=d) for d in range(1, parts)]
    barrier = pltpu.get_barrier_semaphore()
    for partner in partners:
        pl.semaphore_signal(barrier, inc=1, device_id=partner, device_id_type=MESH)

    def copy(number, source, target, device):
        return pltpu.make_async_remote_copy(
            src_ref=source,
            dst_ref=target,
            send_sem=send_sem.at[number],
            recv_sem=recv_sem.at[number],
            device_id=device,
            device_id_type=MESH,
        )

    load_state = pltpu.make_async_copy(state_in, state, load_sem.at[0])
    load_coupling = pltpu.make_async_copy(coupling_in, coupling, load_sem.at[1])
    load_state.start()
    load_coupling.start()

    def sections(sides, edge_pair, targets):
        make_section(
            state,
            scale,
            first,
            second,
            faces[...],
            flips[...],
            sides,
            edge_pair[0],
            edge_pair[1],
            weights,
            section,
            targets,
        )

    load_state.wait()
    pack_edges(state, edges)
    pl.semaphore_wait(barrier, len(partners))
    to_edges = [
        copy(4, edges.at[0], after, place(dx=-1)),
        copy(5, edges.at[1], before, place(dx=1)),
    ]
    to_tables = [
        copy(0, faces, tables.at[0], place(dy=-1)),
        copy(1, flips, tables.at[1], place(dy=-1)),
        copy(2, faces, tables.at[2], place(dy=1)),
        copy(3, flips, tables.at[3], place(dy=1)),
    ]
    for each in to_edges + to_tables:
        each.start()
    def spread_out(part, base, source, target):
        sent = []
        for d in range(1, parts):
            peer = place(dz=d)
            number = base + part * (parts - 1) + d - 1
            sent.append(copy(number, source.at[part, peer[2]], target.at[part, vz], peer))
            sent[-1].start()
        target[part, vz] = source[part, vz]
        return sent

    first_out, first_back = 8, 8 + 2 * (parts - 1)
    count = state.shape[1]
    sections(None, (None, None), (3, 4))
    column_message(section, message.at[0], 0)
    out_0 = spread_out(0, first_out, message, columns)
    for each in to_tables:
        each.wait_recv()
    pack_faces(
        state,
        jnp.concatenate(
            [tables[0, 0:1], tables[1, 0:1], tables[2, 1:2], tables[3, 1:2]], axis=0
        ),
        north_message,
        south_message,
    )
    to_faces = [
        copy(6, north_message, west, place(dy=1)),
        copy(7, south_message, east, place(dy=-1)),
    ]
    for each in to_faces:
        each.start()
    load_coupling.wait()
    factor(coupling, damping, factors)
    for each in to_edges:
        each.wait_recv()
    add_edges(
        scale, second, faces[...], flips[...], before[...], after[...], weights, section, (3, 4)
    )
    column_message(section, patch, 0, only_edges=True)
    to_patches = []
    for d in range(1, parts):
        peer = place(dz=d)
        number = 8 + 4 * (parts - 1) + d - 1
        to_patches.append(copy(number, patch.at[peer[2]], patches.at[vz], peer))
        to_patches[-1].start()
    patches[vz] = patch[vz]
    for each in to_faces:
        each.wait_recv()
    add_sides(scale, first, (west, east), weights, section, (3, 4))
    column_message(section, message.at[1], 1)
    out_1 = spread_out(1, first_out, message, columns)
    for each in out_0 + to_patches:
        each.wait_recv()
    replace_edges(columns.at[0], patches, vz)
    solve(factors, columns.at[0], back.at[0], 0, count)
    back_0 = spread_out(0, first_back, back, returned)
    for each in out_1:
        each.wait_recv()
    solve(factors, columns.at[1], back.at[1], 1, count)
    back_1 = spread_out(1, first_back, back, returned)
    sections((west, east), (before[...], after[...]), (0, 1, 2))
    for each in back_0 + back_1:
        each.wait_recv()
    sent = to_tables + to_edges + to_faces + to_patches + out_0 + out_1 + back_0 + back_1
    for each in sent:
        each.wait_send()


def per_device(
    sizes,
    prognostic,
    metric,
    first_flux,
    second_flux,
    neighbour_face,
    orientation,
    coupling,
    damping,
):
    levels = prognostic.shape[1]
    parts = sizes[2]
    state = prognostic.reshape(FIELDS, levels, 16, LANES)
    scale = metric.reshape(16, LANES)
    faces = neighbour_face.reshape(4, LANES)
    flips = orientation.reshape(4, LANES)
    couples = coupling.reshape(4, levels * parts, 4, LANES)
    damp = damping.reshape(4, LANES)
    copies = 8 + 5 * (parts - 1)
    lanes_out = pltpu.VMEM((parts, ROWS, LANES), jnp.float32)
    tiles = (levels + 3) // 2
    trace = pltpu.VMEM((FIELDS, levels, 4, LANES), jnp.float32)
    column = pltpu.VMEM((2, parts, tiles, 4, LANES), jnp.float32)
    section, returned = pl.pallas_call(
        functools.partial(whole_kernel, sizes),
        out_shape=(f32(FIELDS, levels, 16, LANES), f32(2, parts, tiles, 4, LANES)),
        in_specs=[SM, SM, ANY, VM, VM, VM, ANY, VM, VM],
        out_specs=(VM, VM),
        scratch_shapes=[
            pltpu.VMEM((FIELDS, levels, 16, LANES), jnp.float32),
            pltpu.VMEM((4, levels * parts, 4, LANES), jnp.float32),
            pltpu.VMEM((4, 4, LANES), jnp.int32),
            trace,
            trace,
            pltpu.VMEM((2, 16, LANES), jnp.float32),
            trace,
            trace,
            pltpu.VMEM((16, LANES), jnp.float32),
            pltpu.VMEM((16, LANES), jnp.float32),
            pltpu.VMEM((5, levels * parts // 2, ROWS, LANES), jnp.float32),
            column,
            column,
            column,
            lanes_out,
            lanes_out,
            pltpu.SemaphoreType.DMA((copies,)),
            pltpu.SemaphoreType.DMA((copies,)),
            pltpu.SemaphoreType.DMA((2,)),
        ],
        compiler_params=pltpu.CompilerParams(collective_id=0, has_side_effects=True),
        name="exchange",
    )(
        first_flux,
        second_flux,
        state,
        scale,
        faces,
        flips,
        couples,
        damp,
        jnp.asarray(weight_table()),
    )
    updated = pl.pallas_call(
        finish,
        out_shape=f32(FIELDS, levels, 16, LANES),
        in_specs=[VM, VM],
        out_specs=VM,
        name="finish",
    )(section, returned)
    return updated.reshape(prognostic.shape)


def solution(mesh):
    placed = (
        P(None, "vz", None, None, "hy", "hx"),
        P(None, None, "hy", "hx"),
        P(),
        P(),
        P(None, "hy", "hx"),
        P(None, "hy", "hx"),
        P(None, None, "vz", None, "hy", "hx"),
        P("vz", None, "hy", "hx"),
    )
    sizes = (mesh.shape["hx"], mesh.shape["hy"], mesh.shape["vz"])
    return jax.shard_map(
        functools.partial(per_device, sizes),
        mesh=mesh,
        in_specs=placed,
        out_specs=P(None, "vz", None, None, "hy", "hx"),
        check_vma=False,
    )
```

```python
import functools

import jax
import jax.numpy as jnp
import numpy as np
from jax import lax
from jax.experimental import pallas as pl
from jax.experimental.pallas import tpu as pltpu
from jax.sharding import PartitionSpec as P

step_size = 0.05
lift_weight = 6.0
gravity_couple = 0.5
density_couple = 0.3
theta_couple = 0.4

FIELDS = 5
ROWS = 8
LANES = 128


def derivative_matrix():
    points = np.array([-1.0, -1.0 / np.sqrt(5.0), 1.0 / np.sqrt(5.0), 1.0])
    number = points.shape[0]
    barycentric = np.ones(number)
    for source in range(number):
        for another in range(number):
            if another != source:
                barycentric[source] = barycentric[source] / (points[source] - points[another])
    matrix = np.zeros((number, number))
    for target in range(number):
        for source in range(number):
            if target != source:
                matrix[target, source] = (
                    barycentric[source] / barycentric[target] / (points[target] - points[source])
                )
        matrix[target, target] = -np.sum(matrix[target])
    return matrix


def weight_table():
    d = derivative_matrix()
    half = 0.5 * lift_weight
    along = np.zeros((7, ROWS))
    for row in range(ROWS):
        i = row % 4
        for offset in range(-3, 4):
            if 0 <= i + offset < 4:
                along[offset + 3, row] = -d[i, i + offset]
    cx = np.array([{0: -half, 3: half}.get(r % 4, 0.0) for r in range(ROWS)])
    along[3] += cx
    across = np.zeros((2, 2, 2, ROWS))
    for tile in range(2):
        for other in range(2):
            for row in range(ROWS):
                jl = row // 4
                j = 2 * tile + jl
                across[tile, other, 0, row] = -d[j, 2 * other + jl]
                across[tile, other, 1, row] = -d[j, 2 * other + 1 - jl]
    cy = np.zeros((2, ROWS))
    cy[0, :4] = -half
    cy[1, 4:] = half
    for tile in range(2):
        across[tile, tile, 0] += cy[tile]
    own = np.zeros((2, ROWS))
    for tile in range(2):
        own[tile] = -np.abs(cx) - np.abs(cy[tile])
    rows = np.concatenate(
        [along, across.reshape(8, ROWS), cx[None], np.abs(cx)[None], cy, np.abs(cy), own]
    )
    return np.ascontiguousarray(
        np.broadcast_to(rows[:, :, None], rows.shape + (LANES,)).astype(np.float32)
    )


def rows_of(shape=(ROWS, LANES)):
    return lax.broadcasted_iota(jnp.int32, shape, 0)


def lanes_of(shape=(ROWS, LANES)):
    return lax.broadcasted_iota(jnp.int32, shape, 1)


def spread(row):
    return jnp.broadcast_to(row, (ROWS, LANES))


def node_rows(face, flip):
    k = rows_of() % 4
    k = jnp.where(flip == 1, 3 - k, k)
    return jnp.where(
        face == 0, 4 * k, jnp.where(face == 1, 4 * k + 3, jnp.where(face == 2, k, 12 + k))
    )


def take_rows(tile, index):
    return jnp.take_along_axis(tile, index, axis=0, mode="promise_in_bounds")


def take_nodes(low, high, node):
    index = jnp.where(node >= ROWS, node - ROWS, node)
    return jnp.where(node >= ROWS, take_rows(high, index), take_rows(low, index))


def halves(low, high):
    return jnp.where(rows_of() < 4, low, high)


def pack_faces(state, tables, north_message, south_message):
    levels = state.shape[1]
    node = halves(
        node_rows(spread(tables[0:1]), spread(tables[1:2])),
        node_rows(spread(tables[2:3]), spread(tables[3:4])),
    )

    def at(count, carry):
        for field in range(FIELDS):
            chosen = take_nodes(
                state[field, count, 0:ROWS], state[field, count, ROWS : 2 * ROWS], node
            )
            north_message[field, count] = chosen[0:4]
            south_message[field, count] = chosen[4:8]
        return carry

    lax.fori_loop(0, levels, at, 0, unroll=2)


def pack_edges(state, edges):
    levels = state.shape[1]
    lane = lanes_of()
    zero = state[0, 0, 0:ROWS] - state[0, 0, 0:ROWS]

    def at(count, held):
        held = list(held)
        for field in range(FIELDS):
            number = field * levels + count
            at_first = lane == number
            at_last = lane == lax.rem(number + LANES - 1, LANES)
            for tile in range(2):
                moved = pltpu.roll(
                    state[field, count, tile * ROWS : (tile + 1) * ROWS], number, 1
                )
                held[tile] = jnp.where(at_first, moved, held[tile])
                held[2 + tile] = jnp.where(at_last, moved, held[2 + tile])
        return tuple(held)

    held = lax.fori_loop(0, levels, at, (zero,) * 4)
    for tile in range(2):
        edges[0, tile * ROWS : (tile + 1) * ROWS] = held[tile]
        edges[1, tile * ROWS : (tile + 1) * ROWS] = held[2 + tile]


def edge_values(before, after, faces, flips):
    def lane_value(table, row, lane):
        return jnp.broadcast_to(table[row : row + 1, lane : lane + 1], (ROWS, LANES))

    from_before = take_nodes(
        before[0:ROWS],
        before[ROWS : 2 * ROWS],
        node_rows(lane_value(faces, 2, 0), lane_value(flips, 2, 0)),
    )
    from_after = take_nodes(
        after[0:ROWS],
        after[ROWS : 2 * ROWS],
        node_rows(lane_value(faces, 3, LANES - 1), lane_value(flips, 3, LANES - 1)),
    )
    return halves(pltpu.roll(from_before, 1, 1), pltpu.roll(from_after, LANES - 1, 1))


def make_section(
    state, scale, first, second, faces, flips, sides, before, after, weights, section, targets
):
    levels = state.shape[1]
    node = halves(
        node_rows(
            pltpu.roll(spread(faces[2:3]), LANES - 1, 1),
            pltpu.roll(spread(flips[2:3]), LANES - 1, 1),
        ),
        node_rows(pltpu.roll(spread(faces[3:4]), 1, 1), pltpu.roll(spread(flips[3:4]), 1, 1)),
    )
    edge = None if before is None else edge_values(before, after, faces, flips)
    at_edge = edge_mask()
    place = side_rows()

    def at(count, carry):
        q1 = [[None] * 2 for _ in range(FIELDS)]
        q2 = [[None] * 2 for _ in range(FIELDS)]
        rest = [[None] * 2 for _ in range(FIELDS)]
        own = [[None] * 2 for _ in range(FIELDS)]
        for field in range(FIELDS):
            number = field * levels + count
            tiles = [state[field, count, t * ROWS : (t + 1) * ROWS] for t in range(2)]
            swapped = [pltpu.roll(tile, 4, 0) for tile in tiles]
            chosen = take_nodes(tiles[0], tiles[1], node)
            across = halves(pltpu.roll(chosen, 1, 1), pltpu.roll(chosen, LANES - 1, 1))
            if edge is None:
                across = jnp.where(at_edge, 0.0, across)
            else:
                across = jnp.where(at_edge, edge_level(edge, number), across)
            if sides is not None:
                beside = pair(sides[0][field, count], sides[1][field, count])
            for t in range(2):
                total = weights[3] * tiles[t]
                for offset in (-3, -2, -1, 1, 2, 3):
                    total += weights[offset + 3] * pltpu.roll(tiles[t], (-offset) % ROWS, 0)
                if sides is not None:
                    along = take_rows(beside, place[t])
                    total -= weights[15] * along
                q1[field][t] = total
                total = -weights[17 + t] * across
                for other in range(2):
                    total += weights[7 + 4 * t + 2 * other] * tiles[other]
                    total += weights[8 + 4 * t + 2 * other] * swapped[other]
                q2[field][t] = total
                if field in targets:
                    total = weights[21 + t] * tiles[t] + weights[19 + t] * across
                    if sides is not None:
                        total += weights[16] * along
                    rest[field][t] = total
                    own[field][t] = tiles[t]
        for field in targets:
            for t in range(2):
                total = rest[field][t]
                for other in range(FIELDS):
                    total += first[field, other] * q1[other][t]
                    total += second[field, other] * q2[other][t]
                section[field, count, t * ROWS : (t + 1) * ROWS] = (
                    own[field][t] + step_size * scale[t * ROWS : (t + 1) * ROWS] * total
                )
        return carry

    lax.fori_loop(0, levels, at, 0)


def edge_mask():
    row, lane = rows_of(), lanes_of()
    return ((row < 4) & (lane == 0)) | ((row >= 4) & (lane == LANES - 1))


def edge_level(edge, number):
    return pltpu.roll(edge, lax.rem(2 * LANES - number, LANES), 1)


def add_edges(scale, second, faces, flips, before, after, weights, section, targets):
    levels = section.shape[1]
    edge = edge_values(before, after, faces, flips)
    at_edge = edge_mask()

    def at(count, carry):
        across = [
            jnp.where(at_edge, edge_level(edge, g * levels + count), 0.0) for g in range(FIELDS)
        ]
        for field in targets:
            total = second[field, 0] * across[0]
            for other in range(1, FIELDS):
                total += second[field, other] * across[other]
            for t in range(2):
                span = slice(t * ROWS, (t + 1) * ROWS)
                change = weights[19 + t] * across[field] - weights[17 + t] * total
                section[field, count, span] += step_size * scale[span] * change
        return carry

    lax.fori_loop(0, levels, at, 0, unroll=2)


def side_rows():
    row = rows_of()
    left = row % 4 < 2
    return [jnp.where(left, 2 * tile + row // 4, 4 + 2 * tile + row // 4) for tile in range(2)]


def add_sides(scale, first, sides, weights, section, targets):
    levels = section.shape[1]
    place = side_rows()

    def at(count, carry):
        beside = [pair(sides[0][g, count], sides[1][g, count]) for g in range(FIELDS)]
        for t in range(2):
            span = slice(t * ROWS, (t + 1) * ROWS)
            along = [take_rows(each, place[t]) for each in beside]
            for field in targets:
                total = first[field, 0] * along[0]
                for other in range(1, FIELDS):
                    total += first[field, other] * along[other]
                total = weights[16] * along[field] - weights[15] * total
                section[field, count, span] += step_size * scale[span] * total
        return carry

    lax.fori_loop(0, levels, at, 0, unroll=2)


def point_pair(part):
    return (1, 2) if part == 0 else (0, 3)


def gathered(entries, base, part):
    row = rows_of()
    low, high = point_pair(part)
    total = None
    for m in range(4):
        if entries[m] is None:
            continue
        index = jnp.where(row % 2 == 0, base[m] + low, base[m] + high)
        moved = take_rows(entries[m], index)
        total = moved if total is None else jnp.where(row // 2 == m, moved, total)
    for m in range(4):
        if entries[m] is None:
            total = jnp.where(row // 2 == m, 0.0, total)
    return total


def put_tile(message, p, tile):
    for half in range(2):
        if 2 * p + half < message.shape[0]:
            message[2 * p + half] = tile[4 * half : 4 * half + 4]


def scattered(message, place):
    tile = message[place // 2]
    return take_rows(pair(tile, tile), 2 * (place % 2) + (rows_of() % 4) // 2)


def column_message(section, message, part, only_edges=False):
    levels = section.shape[1]
    lane = lanes_of()
    for t in range(2):
        span = slice(t * ROWS, (t + 1) * ROWS)
        warm = [section[4, count, span] for count in range(levels)]
        entries = []
        for count in range(levels):
            total = section[3, count, span]
            if count + 1 < levels:
                total = total - gravity_couple * warm[count + 1]
            if count > 0:
                total = total + gravity_couple * warm[count - 1]
            entries.append(total)
        entries += [warm[0], warm[levels - 1]]
        entries += [None] * (-len(entries) % 4)
        for side in range(2):
            packed = None
            for p in range(len(entries) // 4):
                tile = gathered(entries[4 * p : 4 * p + 4], [4 * side] * 4, part)
                if only_edges:
                    moved = pltpu.roll(tile, p + t, 1) if p + t else tile
                    packed = moved if p == 0 else jnp.where(lane == p, moved, packed)
                else:
                    put_tile(message.at[2 * t + side], p, tile)
            if only_edges:
                message[2 * t + side] = packed


def replace_edges(columns, patches, j):
    lane = lanes_of((4, LANES))
    target = (j // 2) * (LANES - 1)
    for d in range(columns.shape[0]):
        for p in range((columns.shape[1] + 1) // 2):
            moved = pltpu.roll(patches[d], lax.rem(target + LANES - p, LANES), 1)
            for half in range(2):
                if 2 * p + half < columns.shape[1]:
                    columns[d, 2 * p + half] = jnp.where(
                        lane == target, moved[4 * half : 4 * half + 4], columns[d, 2 * p + half]
                    )


def pair(low, high):
    return jnp.concatenate([low, high], axis=0)


def factor(coupling, damping, factors):
    levels = coupling.shape[1]
    half = levels // 2
    damp = pair(damping[...], damping[...])
    zero = damp - damp

    def at(t, carry):
        far_ratio, far_second, near_ratio, near_second = carry
        up = levels - 1 - t
        entry_a = pair(coupling[0, t], coupling[3, up])
        entry_b = pair(coupling[1, t], coupling[2, up])
        entry_d = pair(coupling[2, t], coupling[1, up])
        entry_e = pair(coupling[3, t], coupling[0, up])
        centre = entry_a + entry_b + entry_d + entry_e + damp
        reduced = entry_a * far_ratio - entry_b
        pivot = centre + entry_a * far_second - reduced * near_ratio
        inverse = 1.0 / pivot
        ratio = -(entry_d + reduced * near_second) * inverse
        second = -entry_e * inverse
        factors[0, t] = inverse
        factors[1, t] = entry_a * inverse
        factors[2, t] = reduced * inverse
        factors[3, t] = ratio
        factors[4, t] = second
        return near_ratio, near_second, ratio, second

    lax.fori_loop(0, half, at, (zero,) * 4)


def solve(factors, columns, message, part, count):
    parts = columns.shape[0]
    levels = parts * count
    half = levels // 2

    def entry_of(d, place):
        return scattered(columns.at[d], place)

    def source(level):
        d, place = level // count, level % count
        entry = entry_of(d, place)
        if place == 0 and d > 0:
            entry = entry + gravity_couple * entry_of(d - 1, count + 1)
        if place == count - 1 and d < parts - 1:
            entry = entry - gravity_couple * entry_of(d + 1, count)
        return entry

    far = near = jnp.zeros((ROWS, LANES), jnp.float32)
    scaled = []
    for t in range(half):
        entry = halves(source(t), source(levels - 1 - t)) * factors[0, t]
        far, near = near, (entry + factors[1, t] * far) - factors[2, t] * near
        scaled.append(near)
    top, under = half - 1, half - 2
    ratio_1, ratio_2 = factors[3, top], factors[3, under]
    second_1, second_2 = factors[4, top], factors[4, under]
    here = 1.0 - second_1 * pltpu.roll(second_2, 4, 0)
    there = ratio_1 - second_1 * pltpu.roll(ratio_2, 4, 0)
    right = scaled[top] - second_1 * pltpu.roll(scaled[under], 4, 0)
    here_2 = pltpu.roll(here, 4, 0)
    there_2 = pltpu.roll(there, 4, 0)
    right_2 = pltpu.roll(right, 4, 0)
    mine = (right * here_2 - there * right_2) / (here * here_2 - there * there_2)
    next_one, next_two = mine, pltpu.roll(mine, 4, 0)
    found = [None] * half
    found[top] = mine
    for t in range(half - 2, -1, -1):
        found[t] = (scaled[t] - factors[4, t] * next_two) - factors[3, t] * next_one
        next_one, next_two = found[t], next_one
    for d in range(parts):
        for p in range((count + 2 + 3) // 4):
            entries, base = [], []
            for m in range(4):
                level = d * count - 1 + 4 * p + m
                inside = 0 <= level < levels and 4 * p + m < count + 2
                low = level < half
                entries.append((found[level] if low else found[levels - 1 - level]) if inside else None)
                base.append(0 if low else 4)
            put_tile(message.at[d], p, gathered(entries, base, part))


def finish(section, returned, updated):
    levels = section.shape[1]
    point = rows_of() % 4
    inner = (point == 1) | (point == 2)
    for t in range(2):
        span = slice(t * ROWS, (t + 1) * ROWS)

        def level(place):
            both = [
                jnp.where(
                    inner,
                    scattered(returned.at[0, 2 * t + side], place),
                    scattered(returned.at[1, 2 * t + side], place),
                )
                for side in range(2)
            ]
            return halves(both[0], both[1])

        speeds = [level(place) for place in range(levels + 2)]
        for count in range(levels):
            jump = speeds[count + 2] - speeds[count]
            updated[0, count, span] = section[0, count, span] - density_couple * jump
            updated[1, count, span] = section[1, count, span]
            updated[2, count, span] = section[2, count, span]
            updated[3, count, span] = speeds[count + 1]
            updated[4, count, span] = section[4, count, span] - theta_couple * jump


VM = pl.BlockSpec(memory_space=pltpu.VMEM)
SM = pl.BlockSpec(memory_space=pltpu.SMEM)
ANY = pl.BlockSpec(memory_space=pl.ANY)
MESH = pl.DeviceIdType.MESH


def f32(*shape):
    return jax.ShapeDtypeStruct(shape, jnp.float32)


def whole_kernel(
    sizes,
    first,
    second,
    state_in,
    scale,
    faces,
    flips,
    coupling_in,
    damping,
    weights,
    section_out,
    returned,
    section,
    state,
    coupling,
    tables,
    north_message,
    south_message,
    edges,
    west,
    east,
    before,
    after,
    factors,
    message,
    columns,
    back,
    patch,
    patches,
    send_sem,
    recv_sem,
    load_sem,
):
    hx, hy, vz = (lax.axis_index(axis) for axis in ("hx", "hy", "vz"))
    size_x, size_y, parts = sizes

    def place(dx=0, dy=0, dz=0):
        return (
            lax.rem(hx + dx + size_x, size_x),
            lax.rem(hy + dy + size_y, size_y),
            lax.rem(vz + dz, parts),
        )

    partners = [place(dx=1), place(dx=-1), place(dy=1), place(dy=-1)]
    partners += [place(dz=d) for d in range(1, parts)]
    barrier = pltpu.get_barrier_semaphore()
    for partner in partners:
        pl.semaphore_signal(barrier, inc=1, device_id=partner, device_id_type=MESH)

    def copy(number, source, target, device):
        return pltpu.make_async_remote_copy(
            src_ref=source,
            dst_ref=target,
            send_sem=send_sem.at[number],
            recv_sem=recv_sem.at[number],
            device_id=device,
            device_id_type=MESH,
        )

    load_state = pltpu.make_async_copy(state_in, state, load_sem.at[0])
    load_coupling = pltpu.make_async_copy(coupling_in, coupling, load_sem.at[1])
    load_state.start()
    load_coupling.start()

    def sections(sides, edge_pair, targets):
        make_section(
            state,
            scale,
            first,
            second,
            faces[...],
            flips[...],
            sides,
            edge_pair[0],
            edge_pair[1],
            weights,
            section,
            targets,
        )

    load_state.wait()
    pack_edges(state, edges)
    pl.semaphore_wait(barrier, len(partners))
    to_edges = [
        copy(4, edges.at[0], after, place(dx=-1)),
        copy(5, edges.at[1], before, place(dx=1)),
    ]
    to_tables = [
        copy(0, faces, tables.at[0], place(dy=-1)),
        copy(1, flips, tables.at[1], place(dy=-1)),
        copy(2, faces, tables.at[2], place(dy=1)),
        copy(3, flips, tables.at[3], place(dy=1)),
    ]
    for each in to_edges + to_tables:
        each.start()
    def spread_out(part, base, source, target):
        sent = []
        for d in range(1, parts):
            peer = place(dz=d)
            number = base + part * (parts - 1) + d - 1
            sent.append(copy(number, source.at[part, peer[2]], target.at[part, vz], peer))
            sent[-1].start()
        target[part, vz] = source[part, vz]
        return sent

    first_out, first_back = 8, 8 + 2 * (parts - 1)
    count = state.shape[1]
    sections(None, (None, None), (3, 4))
    column_message(section, message.at[0], 0)
    out_0 = spread_out(0, first_out, message, columns)
    for each in to_tables:
        each.wait_recv()
    pack_faces(
        state,
        jnp.concatenate(
            [tables[0, 0:1], tables[1, 0:1], tables[2, 1:2], tables[3, 1:2]], axis=0
        ),
        north_message,
        south_message,
    )
    to_faces = [
        copy(6, north_message, west, place(dy=1)),
        copy(7, south_message, east, place(dy=-1)),
    ]
    for each in to_faces:
        each.start()
    load_coupling.wait()
    factor(coupling, damping, factors)
    for each in to_edges:
        each.wait_recv()
    add_edges(
        scale, second, faces[...], flips[...], before[...], after[...], weights, section, (3, 4)
    )
    column_message(section, patch, 0, only_edges=True)
    to_patches = []
    for d in range(1, parts):
        peer = place(dz=d)
        number = 8 + 4 * (parts - 1) + d - 1
        to_patches.append(copy(number, patch.at[peer[2]], patches.at[vz], peer))
        to_patches[-1].start()
    patches[vz] = patch[vz]
    for each in to_faces:
        each.wait_recv()
    add_sides(scale, first, (west, east), weights, section, (3, 4))
    column_message(section, message.at[1], 1)
    out_1 = spread_out(1, first_out, message, columns)
    for each in out_0 + to_patches:
        each.wait_recv()
    replace_edges(columns.at[0], patches, vz)
    solve(factors, columns.at[0], back.at[0], 0, count)
    back_0 = spread_out(0, first_back, back, returned)
    for each in out_1:
        each.wait_recv()
    solve(factors, columns.at[1], back.at[1], 1, count)
    back_1 = spread_out(1, first_back, back, returned)
    sections((west, east), (before[...], after[...]), (0, 1, 2))
    store_section = pltpu.make_async_copy(section, section_out, load_sem.at[2])
    store_section.start()
    for each in back_0 + back_1:
        each.wait_recv()
    sent = to_tables + to_edges + to_faces + to_patches + out_0 + out_1 + back_0 + back_1
    for each in sent:
        each.wait_send()
    store_section.wait()


def per_device(
    sizes,
    prognostic,
    metric,
    first_flux,
    second_flux,
    neighbour_face,
    orientation,
    coupling,
    damping,
):
    levels = prognostic.shape[1]
    parts = sizes[2]
    state = prognostic.reshape(FIELDS, levels, 16, LANES)
    scale = metric.reshape(16, LANES)
    faces = neighbour_face.reshape(4, LANES)
    flips = orientation.reshape(4, LANES)
    couples = coupling.reshape(4, levels * parts, 4, LANES)
    damp = damping.reshape(4, LANES)
    copies = 8 + 5 * (parts - 1)
    lanes_out = pltpu.VMEM((parts, ROWS, LANES), jnp.float32)
    tiles = (levels + 3) // 2
    trace = pltpu.VMEM((FIELDS, levels, 4, LANES), jnp.float32)
    column = pltpu.VMEM((2, parts, tiles, 4, LANES), jnp.float32)
    section, returned = pl.pallas_call(
        functools.partial(whole_kernel, sizes),
        out_shape=(f32(FIELDS, levels, 16, LANES), f32(2, parts, tiles, 4, LANES)),
        in_specs=[SM, SM, ANY, VM, VM, VM, ANY, VM, VM],
        out_specs=(ANY, VM),
        scratch_shapes=[
            pltpu.VMEM((FIELDS, levels, 16, LANES), jnp.float32),
            pltpu.VMEM((FIELDS, levels, 16, LANES), jnp.float32),
            pltpu.VMEM((4, levels * parts, 4, LANES), jnp.float32),
            pltpu.VMEM((4, 4, LANES), jnp.int32),
            trace,
            trace,
            pltpu.VMEM((2, 16, LANES), jnp.float32),
            trace,
            trace,
            pltpu.VMEM((16, LANES), jnp.float32),
            pltpu.VMEM((16, LANES), jnp.float32),
            pltpu.VMEM((5, levels * parts // 2, ROWS, LANES), jnp.float32),
            column,
            column,
            column,
            lanes_out,
            lanes_out,
            pltpu.SemaphoreType.DMA((copies,)),
            pltpu.SemaphoreType.DMA((copies,)),
            pltpu.SemaphoreType.DMA((3,)),
        ],
        compiler_params=pltpu.CompilerParams(collective_id=0, has_side_effects=True),
        name="exchange",
    )(
        first_flux,
        second_flux,
        state,
        scale,
        faces,
        flips,
        couples,
        damp,
        jnp.asarray(weight_table()),
    )
    updated = pl.pallas_call(
        finish,
        out_shape=f32(FIELDS, levels, 16, LANES),
        in_specs=[VM, VM],
        out_specs=VM,
        name="finish",
    )(section, returned)
    return updated.reshape(prognostic.shape)


def solution(mesh):
    placed = (
        P(None, "vz", None, None, "hy", "hx"),
        P(None, None, "hy", "hx"),
        P(),
        P(),
        P(None, "hy", "hx"),
        P(None, "hy", "hx"),
        P(None, None, "vz", None, "hy", "hx"),
        P("vz", None, "hy", "hx"),
    )
    sizes = (mesh.shape["hx"], mesh.shape["hy"], mesh.shape["vz"])
    return jax.shard_map(
        functools.partial(per_device, sizes),
        mesh=mesh,
        in_specs=placed,
        out_specs=P(None, "vz", None, None, "hy", "hx"),
        check_vma=False,
    )
```

```python
import functools

import jax
import jax.numpy as jnp
import numpy as np
from jax import lax
from jax.experimental import pallas as pl
from jax.experimental.pallas import tpu as pltpu
from jax.sharding import PartitionSpec as P

step_size = 0.05
lift_weight = 6.0
gravity_couple = 0.5
density_couple = 0.3
theta_couple = 0.4

FIELDS = 5
ROWS = 8
LANES = 128


def derivative_matrix():
    points = np.array([-1.0, -1.0 / np.sqrt(5.0), 1.0 / np.sqrt(5.0), 1.0])
    number = points.shape[0]
    barycentric = np.ones(number)
    for source in range(number):
        for another in range(number):
            if another != source:
                barycentric[source] = barycentric[source] / (points[source] - points[another])
    matrix = np.zeros((number, number))
    for target in range(number):
        for source in range(number):
            if target != source:
                matrix[target, source] = (
                    barycentric[source] / barycentric[target] / (points[target] - points[source])
                )
        matrix[target, target] = -np.sum(matrix[target])
    return matrix


def weight_table():
    d = derivative_matrix()
    half = 0.5 * lift_weight
    along = np.zeros((7, ROWS))
    for row in range(ROWS):
        i = row % 4
        for offset in range(-3, 4):
            if 0 <= i + offset < 4:
                along[offset + 3, row] = -d[i, i + offset]
    cx = np.array([{0: -half, 3: half}.get(r % 4, 0.0) for r in range(ROWS)])
    along[3] += cx
    across = np.zeros((2, 2, 2, ROWS))
    for tile in range(2):
        for other in range(2):
            for row in range(ROWS):
                jl = row // 4
                j = 2 * tile + jl
                across[tile, other, 0, row] = -d[j, 2 * other + jl]
                across[tile, other, 1, row] = -d[j, 2 * other + 1 - jl]
    cy = np.zeros((2, ROWS))
    cy[0, :4] = -half
    cy[1, 4:] = half
    for tile in range(2):
        across[tile, tile, 0] += cy[tile]
    own = np.zeros((2, ROWS))
    for tile in range(2):
        own[tile] = -np.abs(cx) - np.abs(cy[tile])
    rows = np.concatenate(
        [along, across.reshape(8, ROWS), cx[None], np.abs(cx)[None], cy, np.abs(cy), own]
    )
    return np.ascontiguousarray(
        np.broadcast_to(rows[:, :, None], rows.shape + (LANES,)).astype(np.float32)
    )


def rows_of(shape=(ROWS, LANES)):
    return lax.broadcasted_iota(jnp.int32, shape, 0)


def lanes_of(shape=(ROWS, LANES)):
    return lax.broadcasted_iota(jnp.int32, shape, 1)


def spread(row):
    return jnp.broadcast_to(row, (ROWS, LANES))


def node_rows(face, flip):
    k = rows_of() % 4
    k = jnp.where(flip == 1, 3 - k, k)
    return jnp.where(
        face == 0, 4 * k, jnp.where(face == 1, 4 * k + 3, jnp.where(face == 2, k, 12 + k))
    )


def take_rows(tile, index):
    return jnp.take_along_axis(tile, index, axis=0, mode="promise_in_bounds")


def take_nodes(low, high, node):
    index = jnp.where(node >= ROWS, node - ROWS, node)
    return jnp.where(node >= ROWS, take_rows(high, index), take_rows(low, index))


def halves(low, high):
    return jnp.where(rows_of() < 4, low, high)


def pack_faces(state, tables, north_message, south_message):
    levels = state.shape[1]
    node = halves(
        node_rows(spread(tables[0:1]), spread(tables[1:2])),
        node_rows(spread(tables[2:3]), spread(tables[3:4])),
    )

    def at(count, carry):
        for field in range(FIELDS):
            chosen = take_nodes(
                state[field, count, 0:ROWS], state[field, count, ROWS : 2 * ROWS], node
            )
            north_message[field, count] = chosen[0:4]
            south_message[field, count] = chosen[4:8]
        return carry

    lax.fori_loop(0, levels, at, 0, unroll=2)


def pack_edges(state, edges):
    levels = state.shape[1]
    lane = lanes_of()
    zero = state[0, 0, 0:ROWS] - state[0, 0, 0:ROWS]

    def at(count, held):
        held = list(held)
        for field in range(FIELDS):
            number = field * levels + count
            at_first = lane == number
            at_last = lane == lax.rem(number + LANES - 1, LANES)
            for tile in range(2):
                moved = pltpu.roll(
                    state[field, count, tile * ROWS : (tile + 1) * ROWS], number, 1
                )
                held[tile] = jnp.where(at_first, moved, held[tile])
                held[2 + tile] = jnp.where(at_last, moved, held[2 + tile])
        return tuple(held)

    held = lax.fori_loop(0, levels, at, (zero,) * 4, unroll=4)
    for tile in range(2):
        edges[0, tile * ROWS : (tile + 1) * ROWS] = held[tile]
        edges[1, tile * ROWS : (tile + 1) * ROWS] = held[2 + tile]


def edge_values(before, after, faces, flips):
    def lane_value(table, row, lane):
        return jnp.broadcast_to(table[row : row + 1, lane : lane + 1], (ROWS, LANES))

    from_before = take_nodes(
        before[0:ROWS],
        before[ROWS : 2 * ROWS],
        node_rows(lane_value(faces, 2, 0), lane_value(flips, 2, 0)),
    )
    from_after = take_nodes(
        after[0:ROWS],
        after[ROWS : 2 * ROWS],
        node_rows(lane_value(faces, 3, LANES - 1), lane_value(flips, 3, LANES - 1)),
    )
    return halves(pltpu.roll(from_before, 1, 1), pltpu.roll(from_after, LANES - 1, 1))


def make_section(
    state, scale, first, second, faces, flips, sides, before, after, weights, section, targets
):
    levels = state.shape[1]
    node = halves(
        node_rows(
            pltpu.roll(spread(faces[2:3]), LANES - 1, 1),
            pltpu.roll(spread(flips[2:3]), LANES - 1, 1),
        ),
        node_rows(pltpu.roll(spread(faces[3:4]), 1, 1), pltpu.roll(spread(flips[3:4]), 1, 1)),
    )
    edge = None if before is None else edge_values(before, after, faces, flips)
    at_edge = edge_mask()
    place = side_rows()

    def at(count, carry):
        q1 = [[None] * 2 for _ in range(FIELDS)]
        q2 = [[None] * 2 for _ in range(FIELDS)]
        rest = [[None] * 2 for _ in range(FIELDS)]
        own = [[None] * 2 for _ in range(FIELDS)]
        for field in range(FIELDS):
            number = field * levels + count
            tiles = [state[field, count, t * ROWS : (t + 1) * ROWS] for t in range(2)]
            swapped = [pltpu.roll(tile, 4, 0) for tile in tiles]
            chosen = take_nodes(tiles[0], tiles[1], node)
            across = halves(pltpu.roll(chosen, 1, 1), pltpu.roll(chosen, LANES - 1, 1))
            if edge is None:
                across = jnp.where(at_edge, 0.0, across)
            else:
                across = jnp.where(at_edge, edge_level(edge, number), across)
            if sides is not None:
                beside = pair(sides[0][field, count], sides[1][field, count])
            for t in range(2):
                total = weights[3] * tiles[t]
                for offset in (-3, -2, -1, 1, 2, 3):
                    total += weights[offset + 3] * pltpu.roll(tiles[t], (-offset) % ROWS, 0)
                if sides is not None:
                    along = take_rows(beside, place[t])
                    total -= weights[15] * along
                q1[field][t] = total
                total = -weights[17 + t] * across
                for other in range(2):
                    total += weights[7 + 4 * t + 2 * other] * tiles[other]
                    total += weights[8 + 4 * t + 2 * other] * swapped[other]
                q2[field][t] = total
                if field in targets:
                    total = weights[21 + t] * tiles[t] + weights[19 + t] * across
                    if sides is not None:
                        total += weights[16] * along
                    rest[field][t] = total
                    own[field][t] = tiles[t]
        for field in targets:
            for t in range(2):
                total = rest[field][t]
                for other in range(FIELDS):
                    total += first[field, other] * q1[other][t]
                    total += second[field, other] * q2[other][t]
                section[field, count, t * ROWS : (t + 1) * ROWS] = (
                    own[field][t] + step_size * scale[t * ROWS : (t + 1) * ROWS] * total
                )
        return carry

    lax.fori_loop(0, levels, at, 0)


def edge_mask():
    row, lane = rows_of(), lanes_of()
    return ((row < 4) & (lane == 0)) | ((row >= 4) & (lane == LANES - 1))


def edge_level(edge, number):
    return pltpu.roll(edge, lax.rem(2 * LANES - number, LANES), 1)


def add_edges(scale, second, faces, flips, before, after, weights, section, targets):
    levels = section.shape[1]
    edge = edge_values(before, after, faces, flips)
    at_edge = edge_mask()

    def at(count, carry):
        across = [
            jnp.where(at_edge, edge_level(edge, g * levels + count), 0.0) for g in range(FIELDS)
        ]
        for field in targets:
            total = second[field, 0] * across[0]
            for other in range(1, FIELDS):
                total += second[field, other] * across[other]
            for t in range(2):
                span = slice(t * ROWS, (t + 1) * ROWS)
                change = weights[19 + t] * across[field] - weights[17 + t] * total
                section[field, count, span] += step_size * scale[span] * change
        return carry

    lax.fori_loop(0, levels, at, 0, unroll=2)


def side_rows():
    row = rows_of()
    left = row % 4 < 2
    return [jnp.where(left, 2 * tile + row // 4, 4 + 2 * tile + row // 4) for tile in range(2)]


def add_sides(scale, first, sides, weights, section, targets):
    levels = section.shape[1]
    place = side_rows()

    def at(count, carry):
        beside = [pair(sides[0][g, count], sides[1][g, count]) for g in range(FIELDS)]
        for t in range(2):
            span = slice(t * ROWS, (t + 1) * ROWS)
            along = [take_rows(each, place[t]) for each in beside]
            for field in targets:
                total = first[field, 0] * along[0]
                for other in range(1, FIELDS):
                    total += first[field, other] * along[other]
                total = weights[16] * along[field] - weights[15] * total
                section[field, count, span] += step_size * scale[span] * total
        return carry

    lax.fori_loop(0, levels, at, 0, unroll=2)


def point_pair(part):
    return (1, 2) if part == 0 else (0, 3)


def gathered(entries, base, part):
    row = rows_of()
    low, high = point_pair(part)
    total = None
    for m in range(4):
        if entries[m] is None:
            continue
        index = jnp.where(row % 2 == 0, base[m] + low, base[m] + high)
        moved = take_rows(entries[m], index)
        total = moved if total is None else jnp.where(row // 2 == m, moved, total)
    for m in range(4):
        if entries[m] is None:
            total = jnp.where(row // 2 == m, 0.0, total)
    return total


def put_tile(message, p, tile):
    for half in range(2):
        if 2 * p + half < message.shape[0]:
            message[2 * p + half] = tile[4 * half : 4 * half + 4]


def scattered(message, place):
    tile = message[place // 2]
    return take_rows(pair(tile, tile), 2 * (place % 2) + (rows_of() % 4) // 2)


def column_message(section, message, part, only_edges=False):
    levels = section.shape[1]
    lane = lanes_of()
    for t in range(2):
        span = slice(t * ROWS, (t + 1) * ROWS)
        warm = [section[4, count, span] for count in range(levels)]
        entries = []
        for count in range(levels):
            total = section[3, count, span]
            if count + 1 < levels:
                total = total - gravity_couple * warm[count + 1]
            if count > 0:
                total = total + gravity_couple * warm[count - 1]
            entries.append(total)
        entries += [warm[0], warm[levels - 1]]
        entries += [None] * (-len(entries) % 4)
        for side in range(2):
            packed = None
            for p in range(len(entries) // 4):
                tile = gathered(entries[4 * p : 4 * p + 4], [4 * side] * 4, part)
                if only_edges:
                    moved = pltpu.roll(tile, p + t, 1) if p + t else tile
                    packed = moved if p == 0 else jnp.where(lane == p, moved, packed)
                else:
                    put_tile(message.at[2 * t + side], p, tile)
            if only_edges:
                message[2 * t + side] = packed


def replace_edges(columns, patches, j):
    lane = lanes_of((4, LANES))
    target = (j // 2) * (LANES - 1)
    for d in range(columns.shape[0]):
        for p in range((columns.shape[1] + 1) // 2):
            moved = pltpu.roll(patches[d], lax.rem(target + LANES - p, LANES), 1)
            for half in range(2):
                if 2 * p + half < columns.shape[1]:
                    columns[d, 2 * p + half] = jnp.where(
                        lane == target, moved[4 * half : 4 * half + 4], columns[d, 2 * p + half]
                    )


def pair(low, high):
    return jnp.concatenate([low, high], axis=0)


def factor(coupling, damping, factors):
    levels = coupling.shape[1]
    half = levels // 2
    damp = pair(damping[...], damping[...])
    zero = damp - damp

    def at(t, carry):
        far_ratio, far_second, near_ratio, near_second = carry
        up = levels - 1 - t
        entry_a = pair(coupling[0, t], coupling[3, up])
        entry_b = pair(coupling[1, t], coupling[2, up])
        entry_d = pair(coupling[2, t], coupling[1, up])
        entry_e = pair(coupling[3, t], coupling[0, up])
        centre = entry_a + entry_b + entry_d + entry_e + damp
        reduced = entry_a * far_ratio - entry_b
        pivot = centre + entry_a * far_second - reduced * near_ratio
        inverse = 1.0 / pivot
        ratio = -(entry_d + reduced * near_second) * inverse
        second = -entry_e * inverse
        factors[0, t] = inverse
        factors[1, t] = entry_a * inverse
        factors[2, t] = reduced * inverse
        factors[3, t] = ratio
        factors[4, t] = second
        return near_ratio, near_second, ratio, second

    lax.fori_loop(0, half, at, (zero,) * 4)


def solve(factors, columns, message, part, count):
    parts = columns.shape[0]
    levels = parts * count
    half = levels // 2

    def entry_of(d, place):
        return scattered(columns.at[d], place)

    def source(level):
        d, place = level // count, level % count
        entry = entry_of(d, place)
        if place == 0 and d > 0:
            entry = entry + gravity_couple * entry_of(d - 1, count + 1)
        if place == count - 1 and d < parts - 1:
            entry = entry - gravity_couple * entry_of(d + 1, count)
        return entry

    far = near = jnp.zeros((ROWS, LANES), jnp.float32)
    scaled = []
    for t in range(half):
        entry = halves(source(t), source(levels - 1 - t)) * factors[0, t]
        far, near = near, (entry + factors[1, t] * far) - factors[2, t] * near
        scaled.append(near)
    top, under = half - 1, half - 2
    ratio_1, ratio_2 = factors[3, top], factors[3, under]
    second_1, second_2 = factors[4, top], factors[4, under]
    here = 1.0 - second_1 * pltpu.roll(second_2, 4, 0)
    there = ratio_1 - second_1 * pltpu.roll(ratio_2, 4, 0)
    right = scaled[top] - second_1 * pltpu.roll(scaled[under], 4, 0)
    here_2 = pltpu.roll(here, 4, 0)
    there_2 = pltpu.roll(there, 4, 0)
    right_2 = pltpu.roll(right, 4, 0)
    mine = (right * here_2 - there * right_2) / (here * here_2 - there * there_2)
    next_one, next_two = mine, pltpu.roll(mine, 4, 0)
    found = [None] * half
    found[top] = mine
    for t in range(half - 2, -1, -1):
        found[t] = (scaled[t] - factors[4, t] * next_two) - factors[3, t] * next_one
        next_one, next_two = found[t], next_one
    for d in range(parts):
        for p in range((count + 2 + 3) // 4):
            entries, base = [], []
            for m in range(4):
                level = d * count - 1 + 4 * p + m
                inside = 0 <= level < levels and 4 * p + m < count + 2
                low = level < half
                entries.append((found[level] if low else found[levels - 1 - level]) if inside else None)
                base.append(0 if low else 4)
            put_tile(message.at[d], p, gathered(entries, base, part))


def finish(section, returned, updated):
    levels = section.shape[1]
    point = rows_of() % 4
    inner = (point == 1) | (point == 2)
    for t in range(2):
        span = slice(t * ROWS, (t + 1) * ROWS)

        def level(place):
            both = [
                jnp.where(
                    inner,
                    scattered(returned.at[0, 2 * t + side], place),
                    scattered(returned.at[1, 2 * t + side], place),
                )
                for side in range(2)
            ]
            return halves(both[0], both[1])

        speeds = [level(place) for place in range(levels + 2)]
        for count in range(levels):
            jump = speeds[count + 2] - speeds[count]
            updated[0, count, span] = section[0, count, span] - density_couple * jump
            updated[1, count, span] = section[1, count, span]
            updated[2, count, span] = section[2, count, span]
            updated[3, count, span] = speeds[count + 1]
            updated[4, count, span] = section[4, count, span] - theta_couple * jump


VM = pl.BlockSpec(memory_space=pltpu.VMEM)
SM = pl.BlockSpec(memory_space=pltpu.SMEM)
ANY = pl.BlockSpec(memory_space=pl.ANY)
MESH = pl.DeviceIdType.MESH


def f32(*shape):
    return jax.ShapeDtypeStruct(shape, jnp.float32)


def whole_kernel(
    sizes,
    first,
    second,
    state_in,
    scale,
    faces,
    flips,
    coupling_in,
    damping,
    weights,
    section_out,
    returned,
    section,
    state,
    coupling,
    tables,
    north_message,
    south_message,
    edges,
    west,
    east,
    before,
    after,
    factors,
    message,
    columns,
    back,
    patch,
    patches,
    send_sem,
    recv_sem,
    load_sem,
):
    hx, hy, vz = (lax.axis_index(axis) for axis in ("hx", "hy", "vz"))
    size_x, size_y, parts = sizes

    def place(dx=0, dy=0, dz=0):
        return (
            lax.rem(hx + dx + size_x, size_x),
            lax.rem(hy + dy + size_y, size_y),
            lax.rem(vz + dz, parts),
        )

    partners = [place(dx=1), place(dx=-1), place(dy=1), place(dy=-1)]
    partners += [place(dz=d) for d in range(1, parts)]
    barrier = pltpu.get_barrier_semaphore()
    for partner in partners:
        pl.semaphore_signal(barrier, inc=1, device_id=partner, device_id_type=MESH)

    def copy(number, source, target, device):
        return pltpu.make_async_remote_copy(
            src_ref=source,
            dst_ref=target,
            send_sem=send_sem.at[number],
            recv_sem=recv_sem.at[number],
            device_id=device,
            device_id_type=MESH,
        )

    load_state = pltpu.make_async_copy(state_in, state, load_sem.at[0])
    load_coupling = pltpu.make_async_copy(coupling_in, coupling, load_sem.at[1])
    load_state.start()
    load_coupling.start()

    def sections(sides, edge_pair, targets):
        make_section(
            state,
            scale,
            first,
            second,
            faces[...],
            flips[...],
            sides,
            edge_pair[0],
            edge_pair[1],
            weights,
            section,
            targets,
        )

    load_state.wait()
    pack_edges(state, edges)
    pl.semaphore_wait(barrier, len(partners))
    to_edges = [
        copy(4, edges.at[0], after, place(dx=-1)),
        copy(5, edges.at[1], before, place(dx=1)),
    ]
    to_tables = [
        copy(0, faces, tables.at[0], place(dy=-1)),
        copy(1, flips, tables.at[1], place(dy=-1)),
        copy(2, faces, tables.at[2], place(dy=1)),
        copy(3, flips, tables.at[3], place(dy=1)),
    ]
    for each in to_edges + to_tables:
        each.start()
    def spread_out(part, base, source, target):
        sent = []
        for d in range(1, parts):
            peer = place(dz=d)
            number = base + part * (parts - 1) + d - 1
            sent.append(copy(number, source.at[part, peer[2]], target.at[part, vz], peer))
            sent[-1].start()
        target[part, vz] = source[part, vz]
        return sent

    first_out, first_back = 8, 8 + 2 * (parts - 1)
    count = state.shape[1]
    sections(None, (None, None), (3, 4))
    column_message(section, message.at[0], 0)
    out_0 = spread_out(0, first_out, message, columns)
    for each in to_tables:
        each.wait_recv()
    pack_faces(
        state,
        jnp.concatenate(
            [tables[0, 0:1], tables[1, 0:1], tables[2, 1:2], tables[3, 1:2]], axis=0
        ),
        north_message,
        south_message,
    )
    to_faces = [
        copy(6, north_message, west, place(dy=1)),
        copy(7, south_message, east, place(dy=-1)),
    ]
    for each in to_faces:
        each.start()
    load_coupling.wait()
    factor(coupling, damping, factors)
    for each in to_edges:
        each.wait_recv()
    add_edges(
        scale, second, faces[...], flips[...], before[...], after[...], weights, section, (3, 4)
    )
    column_message(section, patch, 0, only_edges=True)
    to_patches = []
    for d in range(1, parts):
        peer = place(dz=d)
        number = 8 + 4 * (parts - 1) + d - 1
        to_patches.append(copy(number, patch.at[peer[2]], patches.at[vz], peer))
        to_patches[-1].start()
    patches[vz] = patch[vz]
    for each in to_faces:
        each.wait_recv()
    add_sides(scale, first, (west, east), weights, section, (3, 4))
    column_message(section, message.at[1], 1)
    out_1 = spread_out(1, first_out, message, columns)
    for each in out_0 + to_patches:
        each.wait_recv()
    replace_edges(columns.at[0], patches, vz)
    solve(factors, columns.at[0], back.at[0], 0, count)
    back_0 = spread_out(0, first_back, back, returned)
    for each in out_1:
        each.wait_recv()
    solve(factors, columns.at[1], back.at[1], 1, count)
    back_1 = spread_out(1, first_back, back, returned)
    sections((west, east), (before[...], after[...]), (0, 1, 2))
    store_section = pltpu.make_async_copy(section, section_out, load_sem.at[2])
    store_section.start()
    for each in back_0 + back_1:
        each.wait_recv()
    sent = to_tables + to_edges + to_faces + to_patches + out_0 + out_1 + back_0 + back_1
    for each in sent:
        each.wait_send()
    store_section.wait()


def per_device(
    sizes,
    prognostic,
    metric,
    first_flux,
    second_flux,
    neighbour_face,
    orientation,
    coupling,
    damping,
):
    levels = prognostic.shape[1]
    parts = sizes[2]
    state = prognostic.reshape(FIELDS, levels, 16, LANES)
    scale = metric.reshape(16, LANES)
    faces = neighbour_face.reshape(4, LANES)
    flips = orientation.reshape(4, LANES)
    couples = coupling.reshape(4, levels * parts, 4, LANES)
    damp = damping.reshape(4, LANES)
    copies = 8 + 5 * (parts - 1)
    lanes_out = pltpu.VMEM((parts, ROWS, LANES), jnp.float32)
    tiles = (levels + 3) // 2
    trace = pltpu.VMEM((FIELDS, levels, 4, LANES), jnp.float32)
    column = pltpu.VMEM((2, parts, tiles, 4, LANES), jnp.float32)
    section, returned = pl.pallas_call(
        functools.partial(whole_kernel, sizes),
        out_shape=(f32(FIELDS, levels, 16, LANES), f32(2, parts, tiles, 4, LANES)),
        in_specs=[SM, SM, ANY, VM, VM, VM, ANY, VM, VM],
        out_specs=(ANY, VM),
        scratch_shapes=[
            pltpu.VMEM((FIELDS, levels, 16, LANES), jnp.float32),
            pltpu.VMEM((FIELDS, levels, 16, LANES), jnp.float32),
            pltpu.VMEM((4, levels * parts, 4, LANES), jnp.float32),
            pltpu.VMEM((4, 4, LANES), jnp.int32),
            trace,
            trace,
            pltpu.VMEM((2, 16, LANES), jnp.float32),
            trace,
            trace,
            pltpu.VMEM((16, LANES), jnp.float32),
            pltpu.VMEM((16, LANES), jnp.float32),
            pltpu.VMEM((5, levels * parts // 2, ROWS, LANES), jnp.float32),
            column,
            column,
            column,
            lanes_out,
            lanes_out,
            pltpu.SemaphoreType.DMA((copies,)),
            pltpu.SemaphoreType.DMA((copies,)),
            pltpu.SemaphoreType.DMA((3,)),
        ],
        compiler_params=pltpu.CompilerParams(collective_id=0, has_side_effects=True),
        name="exchange",
    )(
        first_flux,
        second_flux,
        state,
        scale,
        faces,
        flips,
        couples,
        damp,
        jnp.asarray(weight_table()),
    )
    updated = pl.pallas_call(
        finish,
        out_shape=f32(FIELDS, levels, 16, LANES),
        in_specs=[VM, VM],
        out_specs=VM,
        name="finish",
    )(section, returned)
    return updated.reshape(prognostic.shape)


def solution(mesh):
    placed = (
        P(None, "vz", None, None, "hy", "hx"),
        P(None, None, "hy", "hx"),
        P(),
        P(),
        P(None, "hy", "hx"),
        P(None, "hy", "hx"),
        P(None, None, "vz", None, "hy", "hx"),
        P("vz", None, "hy", "hx"),
    )
    sizes = (mesh.shape["hx"], mesh.shape["hy"], mesh.shape["vz"])
    return jax.shard_map(
        functools.partial(per_device, sizes),
        mesh=mesh,
        in_specs=placed,
        out_specs=P(None, "vz", None, None, "hy", "hx"),
        check_vma=False,
    )
```
